32 devices in a mesh: expert: 16 (over z, y, x), dp: 2 (over core).
Axes of the slice: x: 2, y: 2, z: 4, core: 2. Of those that a mesh axis runs over, the one named last changes fastest.
Arguments:
- tokens: bfloat16 [768, 2048], P(('expert', 'dp')), may hold values from -6 to 6
- cotangent: bfloat16 [768, 2048], P(('expert', 'dp')), may hold values from -6 to 6
- route_gates: bfloat16 [768, 6], P(('expert', 'dp')), may hold values from 0.049804688 to 1
- routes: int32 [768, 6], P(('expert', 'dp')), may hold values from 0 to 15, all different within a row; in each aligned block of 24 rows (0 to 23, 24 to 47, ...) at most 12 rows name the same one
- w_gate: bfloat16 [16, 1408, 2048], P('expert', 'dp'), may hold values from -0.125 to 0.125
- w_up: bfloat16 [16, 1408, 2048], P('expert', 'dp'), may hold values from -0.125 to 0.125
- w_down: bfloat16 [16, 1408, 2048], P('expert', 'dp'), may hold values from -0.15625 to 0.15625
Outputs:
- layer_out: bfloat16 [768, 2048], P(('expert', 'dp'))
- token_grad: bfloat16 [768, 2048], P(('expert', 'dp'))
- gate_grad: float32 [768, 6], P(('expert', 'dp'))
- grad_gate_proj: float32 [16, 1408, 2048], P('expert', 'dp')
- grad_up_proj: float32 [16, 1408, 2048], P('expert', 'dp')
- grad_down_proj: float32 [16, 1408, 2048], P('expert', 'dp')
The draws below stay inside these ranges and needn't reach their ends.
Inputs may be any that keep to these rules, and one draw needn't show every extreme that they name: `routes`: each row names 6 different experts. In the rows of one device no expert is named by more than 12 rows.
All inputs are finite; a program needn't handle non-finite values.
Results may differ from the reference program's by a relative error of at most 0.01.
Values may be sent and summed in bfloat16 or wider, within the bound.
A program may use at most 128 MiB of HBM per device.

```python
import math
import jax
import jax.numpy as jnp
import numpy as np
from jax import lax

D = 2048
FF = 1408
TOPK = 6
TOK_DEV = 24
EXPERTS = 16
CAP = 12
TOKENS = 768
N_DP = 2


def shard_levels(stream_key, shape, cuts, low, top_value):
    gain, own = 1.0, jax.random.fold_in(stream_key, 6)
    for dim, blocks in cuts:
        draws = jnp.exp(jax.random.uniform(jax.random.fold_in(own, dim), (blocks,), jnp.float32, low / len(cuts), top_value / len(cuts)))
        gain = gain * jnp.repeat(draws, shape[dim] // blocks).reshape([-1 if axis == dim else 1 for axis in range(len(shape))])
    return gain


def routed_block(stream_key, own, number, rows, amount, top, most, lean):
    ranking = jax.random.permutation(stream_key, amount)
    heavy_load, ordinary = load_shares(amount, rows * top, most, lean, True), load_shares(amount, rows * top, most, lean, False)
    places = jnp.arange(amount)

    def named(lengths, offset_by):
        used = int((lengths > 0).sum())
        fixed = max(1, used // 4)
        passed = fixed + (places - fixed + offset_by * (used - fixed)) % max(1, amount - fixed)
        return jnp.zeros((amount,), jnp.int32).at[ranking[jnp.where(places < fixed, places, passed)]].set(jnp.asarray(lengths, jnp.int32))

    lengths = jnp.where(number % 4 == 0, named(heavy_load, number // 4), named(ordinary, number - number // 4 - 1))
    mixed = jax.random.permutation(jax.random.fold_in(own, 3), amount)
    giver, taker = mixed[0:amount // 2 * 2:2], mixed[1:amount // 2 * 2:2]
    slack = jnp.minimum(lengths[giver] - 1, most - lengths[taker]) // 2
    slack = jnp.where((giver == ranking[0]) | (taker == ranking[0]) | (lengths[taker] == 0), 0, jnp.maximum(slack, 0))
    passed = jax.random.randint(jax.random.fold_in(own, 4), (amount // 2,), 0, 1 << 20) % (slack + 1)
    lengths = lengths.at[giver].add(-passed).at[taker].add(passed)
    labels = jnp.searchsorted(jnp.cumsum(lengths), jnp.arange(rows * top), side="right").astype(jnp.int32)
    table = labels.reshape(top, rows).T
    table = table[jax.random.permutation(jax.random.fold_in(own, 1), rows)]
    offset_by = jax.random.randint(jax.random.fold_in(own, 2), (rows, 1), 0, top)
    return jnp.take_along_axis(table, (jnp.arange(top)[None, :] + offset_by) % top, axis=1)


def load_shares(count, total, bound, slope, full):
    loads = [(1 << 20) // math.isqrt(standing ** slope) + 1 for standing in range(1, count + 1)]
    largest = bound if full else min(bound, max(-(-total // count), total * loads[0] // sum(loads)))
    least = 1 if total - largest >= count - 1 else 0
    counts, surplus = [largest] + [least] * (count - 1), total - largest - least * (count - 1)
    while surplus > 0:
        movable = [i for i in range(1, count) if counts[i] < largest] or [i for i in range(1, count) if counts[i] < bound]
        mass, left = sum([loads[i] for i in movable]), surplus
        for i in movable:
            extra = min(bound - counts[i], max(1, left * loads[i] // mass), surplus)
            counts[i] = counts[i] + extra
            surplus = surplus - extra
    return np.array(counts)


def gaussian(stream_key, extent, scale, reach, pieces=(), kind=jnp.bfloat16):
    drawn = scale * jax.random.normal(stream_key, extent, jnp.float32)
    if pieces:
        drawn = drawn * shard_levels(stream_key, extent, pieces, -0.22, 0.18)
    return jnp.clip(drawn, -reach, reach).astype(kind)


def setup_inputs(seed: int = 0) -> dict:
    seeds = jax.random.split(jax.random.key(seed), 8)
    tokens = gaussian(seeds[0], (TOKENS, D), 1.0, 6.0, ((0, 32),))
    cotangent = gaussian(seeds[1], (TOKENS, D), 1.0, 6.0, ((0, 32),))
    route_gates = jnp.clip(jnp.exp(math.log(1.0) - 2.9996462 * jax.random.uniform(seeds[2], (TOKENS, TOPK), jnp.float32) ** shard_levels(seeds[2], (TOKENS, TOPK), ((0, 32),), -0.2, 0.2)), 0.049804688, 1.0).astype(jnp.bfloat16)
    routes_keys = jax.random.split(jax.random.fold_in(seeds[3], 1), TOKENS // TOK_DEV)
    routes_turns = jax.random.permutation(jax.random.fold_in(seeds[3], 3), TOKENS // TOK_DEV)
    routes = jax.vmap(lambda own, number: routed_block(jax.random.fold_in(seeds[3], 2), own, number, TOK_DEV, EXPERTS, TOPK, CAP, 2))(routes_keys, routes_turns).reshape((TOKENS, TOPK))
    w_gate = gaussian(seeds[4], (EXPERTS, FF, D), D ** -0.5, 0.125, ((0, 16), (1, 2)))
    w_up = gaussian(seeds[5], (EXPERTS, FF, D), D ** -0.5, 0.125, ((0, 16), (1, 2)))
    w_down = gaussian(seeds[6], (EXPERTS, FF, D), FF ** -0.5, 0.15625, ((0, 16), (1, 2)))
    return dict(tokens=tokens, cotangent=cotangent, route_gates=route_gates, routes=routes, w_gate=w_gate, w_up=w_up, w_down=w_down)


def expert_rows(rows_in, rows_back, gate_proj, up_proj, down_proj):
    row_count = rows_in.shape[0]
    hidden_shard = FF // N_DP
    inner = (((1,), (1,)), ((), ()))
    outer = (((0,), (0,)), ((), ()))
    gate_pre = lax.dot_general(rows_in, gate_proj, inner, preferred_element_type=jnp.float32)
    up_pre = lax.dot_general(rows_in, up_proj, inner, preferred_element_type=jnp.float32)
    sigmoid_gate = jax.nn.sigmoid(gate_pre)
    hidden = (gate_pre * sigmoid_gate * up_pre).astype(jnp.bfloat16)
    parts = jnp.einsum("rjf,jfd->rjd", hidden.astype(jnp.float32).reshape(row_count, N_DP, hidden_shard),
                       down_proj.astype(jnp.float32).reshape(N_DP, hidden_shard, D)).astype(jnp.bfloat16)
    summed_out = jnp.sum(parts.astype(jnp.float32), axis=1)
    back_hidden = jnp.dot(rows_back, down_proj.T, preferred_element_type=jnp.float32)
    grad_pre = (back_hidden * up_pre * sigmoid_gate * (1.0 + gate_pre * (1.0 - sigmoid_gate))).astype(jnp.bfloat16)
    grad_upv = (back_hidden * gate_pre * sigmoid_gate).astype(jnp.bfloat16)
    grad_down = jnp.dot(hidden.T, rows_back, preferred_element_type=jnp.float32)
    grad_gate = lax.dot_general(grad_pre, rows_in, outer, preferred_element_type=jnp.float32)
    grad_up = lax.dot_general(grad_upv, rows_in, outer, preferred_element_type=jnp.float32)
    token_parts = jnp.einsum("rjf,jfd->rjd", grad_pre.astype(jnp.float32).reshape(row_count, N_DP, hidden_shard),
                             gate_proj.astype(jnp.float32).reshape(N_DP, hidden_shard, D))
    token_parts = token_parts + jnp.einsum("rjf,jfd->rjd", grad_upv.astype(jnp.float32).reshape(row_count, N_DP, hidden_shard),
                                           up_proj.astype(jnp.float32).reshape(N_DP, hidden_shard, D))
    summed_back = jnp.sum(token_parts.astype(jnp.bfloat16).astype(jnp.float32), axis=1)
    return summed_out, summed_back, grad_gate, grad_up, grad_down


def reference(tokens, cotangent, route_gates, routes, w_gate, w_up, w_down):
    token_count = tokens.shape[0]
    blocks = token_count // TOK_DEV
    per_block = TOK_DEV * TOPK
    flat_routes = routes.reshape(blocks, per_block)
    onehot = (flat_routes[:, :, None] == jnp.arange(EXPERTS, dtype=jnp.int32)[None, None, :]).astype(jnp.int32)
    before = jnp.cumsum(onehot, axis=1) - onehot
    slot_rank = jnp.sum(before * onehot, axis=2)
    block_ids = jnp.arange(blocks, dtype=jnp.int32)[:, None]
    target = (flat_routes * blocks + block_ids) * CAP + slot_rank
    source = jnp.arange(token_count * TOPK, dtype=jnp.int32).reshape(blocks, per_block)
    sentinel = token_count * TOPK
    slot_source = jnp.full((EXPERTS * blocks * CAP,), sentinel, dtype=jnp.int32)
    slot_source = slot_source.at[target.reshape(-1)].set(source.reshape(-1)).reshape(EXPERTS, blocks * CAP)
    token_table = jnp.concatenate([tokens, jnp.zeros((1, D), tokens.dtype)], axis=0)
    scaled = (route_gates.astype(jnp.float32)[:, :, None] * cotangent.astype(jnp.float32)[:, None, :]).astype(jnp.bfloat16)
    scaled_table = jnp.concatenate([scaled.reshape(token_count * TOPK, D), jnp.zeros((1, D), scaled.dtype)], axis=0)

    def per_expert(operands):
        slot_ids, gate_proj, up_proj, down_proj = operands
        return expert_rows(token_table[slot_ids // TOPK], scaled_table[slot_ids], gate_proj, up_proj, down_proj)

    summed_out, summed_back, grad_gate, grad_up, grad_down = lax.map(per_expert, (slot_source, w_gate, w_up, w_down))
    flat_ids = slot_source.reshape(-1)
    route_out = jnp.zeros((token_count * TOPK + 1, D), jnp.float32).at[flat_ids].set(summed_out.reshape(-1, D))
    route_out = route_out[:-1].reshape(token_count, TOPK, D)
    route_back = jnp.zeros((token_count * TOPK + 1, D), jnp.float32).at[flat_ids].set(summed_back.reshape(-1, D))
    route_back = route_back[:-1].reshape(token_count, TOPK, D)
    layer_out = jnp.sum(route_gates.astype(jnp.float32)[:, :, None] * route_out, axis=1).astype(jnp.bfloat16)
    gate_grad = jnp.sum(cotangent.astype(jnp.float32)[:, None, :] * route_out, axis=2)
    token_grad = jnp.sum(route_back, axis=1).astype(jnp.bfloat16)
    return (layer_out, token_grad, gate_grad, grad_gate, grad_up, grad_down)
```

```python
import functools

import jax
import jax.numpy as jnp
from jax import lax
from jax.experimental import pallas as pl
from jax.experimental.pallas import tpu as pltpu
from jax.sharding import PartitionSpec as P

INNER = (((1,), (1,)), ((), ()))
OUTER = (((0,), (0,)), ((), ()))
LANES = 128
VMEM_LIMIT = 60 * 1024 * 1024


def dot_f32(left, right, dims=(((1,), (0,)), ((), ()))):
    return lax.dot_general(left, right, dims, preferred_element_type=jnp.float32)


class Net:
    def __init__(self, depth, group, send_sem, recv_sem):
        me, core = lax.axis_index("expert"), lax.axis_index("dp")
        z, y, x = me // 4, (me // 2) % 2, me % 2
        self.me, self.core, self.z, self.y, self.x = me, core, z, y, x

        def at(zz, yy, xx, cc):
            return (zz * 4 + yy * 2 + xx, cc)

        self.deep = [at((z + k) % depth, y, x, core) for k in range(1, depth)]
        self.across, self.beside = at(z, 1 - y, x, core), at(z, y, 1 - x, core)
        self.mates = [at(z, y, x, (core + k) % group) for k in range(1, group)]
        self.across_id, self.beside_id = self.across[0], self.beside[0]
        self.send_sem, self.recv_sem = send_sem, recv_sem
        self.sent, self.used = [], 0

    def barrier(self):
        peers = self.deep + [self.across, self.beside] + self.mates
        barrier = pltpu.get_barrier_semaphore()
        for peer in peers:
            pl.semaphore_signal(barrier, inc=1, device_id=peer, device_id_type=pl.DeviceIdType.MESH)
        pl.semaphore_wait(barrier, len(peers))

    def push(self, src, dst, peer):
        index = self.used
        self.used += 1
        copy = pltpu.make_async_remote_copy(
            src_ref=src, dst_ref=dst, send_sem=self.send_sem.at[index], recv_sem=self.recv_sem.at[index],
            device_id=peer, device_id_type=pl.DeviceIdType.MESH,
        )
        copy.start()
        self.sent.append(copy)
        return copy

    def finish(self):
        for copy in self.sent:
            copy.wait_send()


def arrived(copies):
    for copy in copies:
        copy.wait_recv()


def flat(value):
    return value.reshape(-1, value.shape[-1])


def dispatch_kernel(depth, group, top, *refs):
    (rt, tok, cot, tri, kcap), (row_rt, row_tok, row_cot, tabs) = refs[:5], refs[5:9]
    (z_rt, z_tok, z_cot, y_rt, y_tok, y_cot, x_rt, x_tok, x_cot) = refs[9:18]
    (f_rt, f0_tok, f0_cot, f1_tok, f1_cot) = refs[18:23]
    own_sem, send_sem, recv_sem = refs[23:]
    net = Net(depth, group, send_sem, recv_sem)
    z, y, x, core = net.z, net.y, net.x, net.core
    half = tok.shape[1] // 2
    low, high = pl.ds(0, half), pl.ds(half, half)
    span = row_rt.shape[3]
    net.barrier()

    own = []
    for i, (src, dst) in enumerate(((rt, z_rt), (tok, z_tok), (cot, z_cot))):
        copy = pltpu.make_async_copy(src, dst.at[z], own_sem.at[i])
        copy.start()
        own.append(copy)
    deep_rt = [net.push(rt, z_rt.at[z], peer) for peer in net.deep]
    deep_tok = [net.push(tok, z_tok.at[z], peer) for peer in net.deep]
    for copy in own:
        copy.wait()
    arrived(deep_rt)
    side_rt = [net.push(z_rt, y_rt, net.across), net.push(z_rt, x_rt, net.beside)]
    arrived(deep_tok)
    up_tok = net.push(z_tok.at[:, :, low], y_tok, net.across)
    by_tok = net.push(z_tok.at[:, :, high], x_tok, net.beside)
    deep_cot = [net.push(cot, z_cot.at[z], peer) for peer in net.deep]
    arrived(side_rt)

    lane = lax.broadcasted_iota(jnp.int32, (kcap.shape[0], LANES), 1)

    def table(which, part, source, expert, base):
        routing = flat(source[...]).astype(jnp.float32)
        named = (routing == expert.astype(jnp.float32)) & (lane < top)
        used = jnp.sum(named.astype(jnp.float32), axis=1, keepdims=True)
        used = jnp.broadcast_to(used, lane.shape)
        rank = dot_f32(tri[...], used.astype(jnp.bfloat16))
        slot = rank + kcap[...] + (base * span).astype(jnp.float32)
        hit = (used > 0.5) & (slot == lane.astype(jnp.float32))
        tabs[which, part] = hit.astype(jnp.float32).astype(jnp.bfloat16)

    table(0, 0, z_rt, net.me, y)
    table(0, 1, y_rt, net.me, 1 - y)
    table(1, 0, z_rt, net.beside_id, y)
    table(1, 1, y_rt, net.beside_id, 1 - y)
    table(2, 0, z_rt, net.me, x)
    table(2, 1, x_rt, net.me, 1 - x)
    table(3, 0, z_rt, net.across_id, x)
    table(3, 1, x_rt, net.across_id, 1 - x)

    def chosen(which, near, far):
        rows = dot_f32(tabs[which, 0], flat(near), OUTER) + dot_f32(tabs[which, 1], flat(far), OUTER)
        return rows[: 2 * span].astype(jnp.bfloat16).reshape(2, span, -1)

    def share(view):
        return [net.push(view, view, peer) for peer in net.mates]

    def first_way(near, far, send, rows, cols):
        send[...] = chosen(1, near, far)
        moved = net.push(send, rows.at[core, x, :, :, cols], net.beside)
        rows[core, x, :, :, cols] = chosen(0, near, far)
        return moved, share(rows.at[core, x, :, :, cols])

    def second_way(near, far, send, rows, cols):
        send[...] = chosen(3, near, far)
        moved = net.push(send, rows.at[core, :, y, :, cols], net.across)
        rows[core, :, y, :, cols] = chosen(2, near, far)
        return moved, share(rows.at[core, :, y, :, cols])

    pending = []
    every = pl.ds(0, LANES)
    moved_rt, shared = first_way(z_rt[...], y_rt[...], f_rt, row_rt, every)
    pending += shared
    up_tok.wait_recv()
    moved_low, shared = first_way(z_tok[:, :, low], y_tok[...], f0_tok, row_tok, low)
    pending += shared
    by_tok.wait_recv()
    moved_high, shared = second_way(z_tok[:, :, high], x_tok[...], f1_tok, row_tok, high)
    pending += shared
    arrived(deep_cot)
    up_cot = net.push(z_cot.at[:, :, low], y_cot, net.across)
    by_cot = net.push(z_cot.at[:, :, high], x_cot, net.beside)
    moved_rt.wait_recv()
    pending += share(row_rt.at[core, 1 - x])
    moved_low.wait_recv()
    pending += share(row_tok.at[core, 1 - x, :, :, low])
    moved_high.wait_recv()
    pending += share(row_tok.at[core, :, 1 - y, :, high])
    up_cot.wait_recv()
    moved_low, shared = first_way(z_cot[:, :, low], y_cot[...], f0_cot, row_cot, low)
    pending += shared
    by_cot.wait_recv()
    moved_high, shared = second_way(z_cot[:, :, high], x_cot[...], f1_cot, row_cot, high)
    pending += shared
    moved_low.wait_recv()
    pending += share(row_cot.at[core, 1 - x, :, :, low])
    moved_high.wait_recv()
    pending += share(row_cot.at[core, :, 1 - y, :, high])
    arrived(pending)
    net.finish()


def dispatch(experts, group, top, capacity, routing, tokens, cotangent):
    depth = experts // 4
    count, width = tokens.shape
    span, half = depth * capacity, width // 2
    bf16 = jnp.bfloat16
    order = jnp.arange(depth * count, dtype=jnp.int32)
    block = order // count
    tri = ((order[None, :] < order[:, None]) & (block[None, :] == block[:, None])).astype(bf16)
    kcap = jnp.broadcast_to((block * capacity).astype(jnp.float32)[:, None], (depth * count, LANES))
    vmem = pl.BlockSpec(memory_space=pltpu.VMEM)
    dense = [pltpu.VMEM((depth, count, w), bf16) for w in (LANES, width, width) + (LANES, half, half) * 2]
    routed = [pltpu.VMEM((2, span, w), bf16) for w in (LANES, half, half, half, half)]
    copies = 3 * (depth - 1) + 6 + 5 + 10 * (group - 1)
    return pl.pallas_call(
        functools.partial(dispatch_kernel, depth, group, top),
        out_shape=[
            jax.ShapeDtypeStruct((group, 2, 2, span, LANES), bf16),
            jax.ShapeDtypeStruct((group, 2, 2, span, width), bf16),
            jax.ShapeDtypeStruct((group, 2, 2, span, width), bf16),
            jax.ShapeDtypeStruct((4, 2, depth * count, LANES), bf16),
        ],
        in_specs=[vmem] * 5,
        out_specs=[vmem] * 4,
        scratch_shapes=dense + routed + [
            pltpu.SemaphoreType.DMA((3,)),
            pltpu.SemaphoreType.DMA((copies,)),
            pltpu.SemaphoreType.DMA((copies,)),
        ],
        compiler_params=pltpu.CompilerParams(
            collective_id=0, has_side_effects=True, vmem_limit_bytes=VMEM_LIMIT
        ),
    )(routing, tokens, cotangent, tri, kcap)


JOBS = ((0, 0), (1, 0), (1, 1), (2, 0), (2, 1))


def combine_kernel(depth, group, *refs):
    tabs, parts, outs = refs[0], refs[1:4], refs[4:7]
    bufs = refs[7 : 7 + 8 * len(JOBS)]
    send_sem, recv_sem = refs[7 + 8 * len(JOBS) :]
    net = Net(depth, group, send_sem, recv_sem)
    z, y, x, core = net.z, net.y, net.x, net.core
    net.barrier()

    class Job:
        pass

    jobs = []
    for number, (source, kind) in enumerate(JOBS):
        job = Job()
        job.part, job.out, job.kind = parts[source], outs[source], kind
        (job.mate, job.give, job.own, job.take, job.far, job.near, job.came, job.deep) = bufs[8 * number : 8 * number + 8]
        width = job.give.shape[-1]
        job.cols = pl.ds(kind * width, width)
        job.first, job.second = (net.beside, net.across) if kind == 0 else (net.across, net.beside)
        job.tabs = 2 * kind
        jobs.append(job)

    def pick(ref, lead, job, remote, cols):
        if job.kind == 0:
            return ref.at[lead, 1 - x if remote else x, :, :, cols]
        return ref.at[lead, :, 1 - y if remote else y, :, cols]

    every = lambda job: pl.ds(0, job.give.shape[-1])

    def exchange(job, remote):
        return [
            net.push(pick(job.part, (core + k) % group, job, remote, job.cols), pick(job.mate, k - 1, job, remote, every(job)), net.mates[k - 1])
            for k in range(1, group)
        ]

    def total(job, remote):
        acc = pick(job.part, core, job, remote, job.cols)[...].astype(jnp.float32)
        for k in range(1, group):
            acc = acc + pick(job.mate, k - 1, job, remote, every(job))[...].astype(jnp.float32)
        return acc.astype(jnp.bfloat16)

    def spread(job, part):
        rows = 2 * job.give.shape[1]
        mine = dot_f32(tabs[job.tabs, part, :, :rows], flat(job.own[...]))
        theirs = dot_f32(tabs[job.tabs + 1, part, :, :rows], flat(job.take[...]))
        return (mine + theirs).reshape(job.far.shape)

    for job in jobs:
        job.m1 = exchange(job, True)
    for job in jobs:
        job.m0 = exchange(job, False)
    for job in jobs:
        arrived(job.m1)
        job.give[...] = total(job, True)
        job.c1 = net.push(job.give, job.take, job.first)
    for job in jobs:
        arrived(job.m0)
        job.own[...] = total(job, False)
    for job in jobs:
        job.c1.wait_recv()
        job.far[...] = spread(job, 1).astype(jnp.bfloat16)
        job.c2 = net.push(job.far, job.came, job.second)
        job.near[...] = spread(job, 0).astype(jnp.bfloat16)
    for job in jobs:
        job.c2.wait_recv()
        job.near[...] = (job.near[...].astype(jnp.float32) + job.came[...].astype(jnp.float32)).astype(jnp.bfloat16)
        job.c3 = [
            net.push(job.near.at[(z + k) % depth], job.deep.at[z], net.deep[k - 1]) for k in range(1, depth)
        ]
    for job in jobs:
        arrived(job.c3)
        acc = job.near[z].astype(jnp.float32)
        for k in range(1, depth):
            acc = acc + job.deep[(z + k) % depth].astype(jnp.float32)
        job.out[:, job.cols] = acc.astype(job.out.dtype)
    net.finish()


def combine(experts, group, capacity, count, tabs, parts):
    depth = experts // 4
    width = parts[1].shape[-1]
    span, half = depth * capacity, width // 2
    bf16 = jnp.bfloat16
    vmem = pl.BlockSpec(memory_space=pltpu.VMEM)
    bufs = []
    for source, kind in JOBS:
        w = LANES if source == 0 else half
        bufs += [pltpu.VMEM((max(1, group - 1), 2, 2, span, w), bf16)]
        bufs += [pltpu.VMEM((2, span, w), bf16)] * 3
        bufs += [pltpu.VMEM((depth, count, w), bf16)] * 4
    copies = len(JOBS) * (2 * (group - 1) + 2 + depth - 1)
    return pl.pallas_call(
        functools.partial(combine_kernel, depth, group),
        out_shape=[
            jax.ShapeDtypeStruct((count, LANES), jnp.float32),
            jax.ShapeDtypeStruct((count, width), bf16),
            jax.ShapeDtypeStruct((count, width), bf16),
        ],
        in_specs=[vmem] * 4,
        out_specs=[vmem] * 3,
        scratch_shapes=bufs + [
            pltpu.SemaphoreType.DMA((copies,)),
            pltpu.SemaphoreType.DMA((copies,)),
        ],
        compiler_params=pltpu.CompilerParams(
            collective_id=1, has_side_effects=True, vmem_limit_bytes=VMEM_LIMIT
        ),
    )(tabs, *parts)


def per_device(tokens, cotangent, route_gates, routes, w_gate, w_up, w_down):
    experts, group = lax.axis_size("expert"), lax.axis_size("dp")
    token_count, top_count = routes.shape
    width = tokens.shape[1]
    capacity = max(2, token_count * top_count * 4 // (3 * experts))
    slots = experts * group * capacity
    gate_shard, up_shard, down_shard = (w_gate[0], w_up[0], w_down[0])
    me = lax.axis_index("expert")

    routing = jnp.concatenate([routes.astype(jnp.bfloat16), route_gates], axis=1)
    routing = jnp.pad(routing, ((0, 0), (0, LANES - 2 * top_count)))
    row_rt, row_tok, row_cot, tabs = dispatch(experts, group, top_count, capacity, routing, tokens, cotangent)
    shape = row_tok.shape
    row_rt = row_rt.reshape(slots, LANES).astype(jnp.float32)
    rows_in, rows_cot = row_tok.reshape(slots, width), row_cot.reshape(slots, width)
    named = row_rt[:, :top_count] == me.astype(jnp.float32)
    row_gate = jnp.sum(jnp.where(named, row_rt[:, top_count : 2 * top_count], 0.0), axis=1)[:, None]

    gate_pre = dot_f32(rows_in, gate_shard, INNER)
    up_pre = dot_f32(rows_in, up_shard, INNER)
    sig = jax.nn.sigmoid(gate_pre)
    hidden = (gate_pre * sig * up_pre).astype(jnp.bfloat16)
    out_rows = dot_f32(hidden, down_shard)
    row_grad = jnp.sum(out_rows * rows_cot.astype(jnp.float32), axis=1)[:, None]
    out_part = (out_rows * row_gate).astype(jnp.bfloat16)
    lane = jnp.arange(LANES, dtype=jnp.int32)[None, :]
    row_high = row_grad.astype(jnp.bfloat16)
    row_low = (row_grad - row_high.astype(jnp.float32)).astype(jnp.bfloat16)
    zero = jnp.zeros((), jnp.bfloat16)
    grad_cols = jnp.where(lane == me, row_high, jnp.where(lane == LANES // 2 + me, row_low, zero))
    rows_back = (rows_cot.astype(jnp.float32) * row_gate).astype(jnp.bfloat16)
    back_hidden = dot_f32(rows_back, down_shard, INNER)
    grad_pre = (back_hidden * up_pre * sig * (1.0 + gate_pre * (1.0 - sig))).astype(jnp.bfloat16)
    grad_upv = (back_hidden * gate_pre * sig).astype(jnp.bfloat16)
    back_part = (dot_f32(grad_pre, gate_shard) + dot_f32(grad_upv, up_shard)).astype(jnp.bfloat16)
    gate_cols, mixed, token_grad = combine(
        experts, group, capacity, token_count, tabs,
        [grad_cols.reshape(shape[:4] + (LANES,)), out_part.reshape(shape), back_part.reshape(shape)],
    )
    grad_down = dot_f32(hidden, rows_back, OUTER)
    grad_gate = dot_f32(grad_pre, rows_in, OUTER)
    grad_up = dot_f32(grad_upv, rows_in, OUTER)
    column = lane[:, None, :] % (LANES // 2)
    gate_grad = jnp.sum(jnp.where(routes[:, :, None] == column, gate_cols[:, None, :], 0.0), axis=2)
    return (mixed, token_grad, gate_grad, grad_gate[None], grad_up[None], grad_down[None])


def solution(mesh):
    row = P(("expert", "dp"), None)
    wide = P("expert", "dp", None)
    return jax.shard_map(
        per_device,
        mesh=mesh,
        in_specs=(row, row, row, row, wide, wide, wide),
        out_specs=(row, row, row, wide, wide, wide),
        check_vma=False,
    )
```

```python
import functools

import jax
import jax.numpy as jnp
from jax import lax
from jax.experimental import pallas as pl
from jax.experimental.pallas import tpu as pltpu
from jax.sharding import PartitionSpec as P

INNER = (((1,), (1,)), ((), ()))
OUTER = (((0,), (0,)), ((), ()))
LANES = 128
VMEM_LIMIT = 60 * 1024 * 1024
FUSED_LIMIT = 4 * 1024 * 1024


def dot_f32(left, right, dims=(((1,), (0,)), ((), ()))):
    return lax.dot_general(left, right, dims, preferred_element_type=jnp.float32)


class Net:
    def __init__(self, depth, group, send_sem, recv_sem):
        me, core = lax.axis_index("expert"), lax.axis_index("dp")
        z, y, x = me // 4, (me // 2) % 2, me % 2
        self.me, self.core, self.z, self.y, self.x = me, core, z, y, x

        def at(zz, yy, xx, cc):
            return (zz * 4 + yy * 2 + xx, cc)

        self.deep = [at((z + k) % depth, y, x, core) for k in range(1, depth)]
        self.across, self.beside = at(z, 1 - y, x, core), at(z, y, 1 - x, core)
        self.mates = [at(z, y, x, (core + k) % group) for k in range(1, group)]
        self.across_id, self.beside_id = self.across[0], self.beside[0]
        self.send_sem, self.recv_sem = send_sem, recv_sem
        self.sent, self.used = [], 0

    def barrier(self):
        peers = self.deep + [self.across, self.beside] + self.mates
        barrier = pltpu.get_barrier_semaphore()
        for peer in peers:
            pl.semaphore_signal(barrier, inc=1, device_id=peer, device_id_type=pl.DeviceIdType.MESH)
        pl.semaphore_wait(barrier, len(peers))

    def push(self, src, dst, peer):
        index = self.used
        self.used += 1
        copy = pltpu.make_async_remote_copy(
            src_ref=src, dst_ref=dst, send_sem=self.send_sem.at[index], recv_sem=self.recv_sem.at[index],
            device_id=peer, device_id_type=pl.DeviceIdType.MESH,
        )
        copy.start()
        self.sent.append(copy)
        return copy

    def finish(self):
        for copy in self.sent:
            copy.wait_send()


def arrived(copies):
    for copy in copies:
        copy.wait_recv()


def flat(value):
    return value.reshape(-1, value.shape[-1])


class Dispatch:
    def __init__(self, net, top, ins, rows, tabs, dense, routed, own_sem):
        self.net, self.top, self.ins, self.rows, self.tabs = net, top, ins, rows, tabs
        self.near, self.up, self.by = dense[:3], dense[3:6], dense[6:9]
        self.send0, self.send1 = (routed[0], routed[1], routed[2]), (None, routed[3], routed[4])
        self.own_sem = own_sem
        half = ins[1].shape[1] // 2
        self.low = (pl.ds(0, LANES), pl.ds(0, half), pl.ds(0, half))
        self.high = pl.ds(half, half)
        self.span = rows[0].shape[3]
        self.pending = []
        self.moved0, self.moved1, self.deep, self.side0, self.side1 = {}, {}, {}, {}, {}

    def start(self):
        net = self.net
        own = []
        for t in range(3):
            copy = pltpu.make_async_copy(self.ins[t], self.near[t].at[net.z], self.own_sem.at[t])
            copy.start()
            own.append(copy)
        self.push_deep(0)
        self.push_deep(1)
        for copy in own:
            copy.wait()

    def push_deep(self, t):
        net = self.net
        self.deep[t] = [net.push(self.ins[t], self.near[t].at[net.z], peer) for peer in net.deep]

    def push_side(self, t):
        net = self.net
        arrived(self.deep[t])
        if t == 0:
            self.side0[t] = net.push(self.near[t], self.up[t], net.across)
            self.side1[t] = net.push(self.near[t], self.by[t], net.beside)
        else:
            self.side0[t] = net.push(self.near[t].at[:, :, self.low[t]], self.up[t], net.across)
            self.side1[t] = net.push(self.near[t].at[:, :, self.high], self.by[t], net.beside)

    def tables(self):
        net, span, count = self.net, self.span, self.ins[0].shape[0]
        self.side0[0].wait_recv()
        self.side1[0].wait_recv()
        depth = self.near[0].shape[0]
        total = depth * count
        lane = lax.broadcasted_iota(jnp.int32, (total, LANES), 1)
        row = lax.broadcasted_iota(jnp.int32, (total, LANES), 0)
        down, right = lax.broadcasted_iota(jnp.int32, (total, total), 0), lax.broadcasted_iota(jnp.int32, (total, total), 1)
        kcap = jnp.zeros((total, LANES), jnp.int32)
        first = jnp.zeros((total, total), jnp.int32)
        for k in range(1, depth):
            kcap = jnp.where(row >= k * count, k * (span // depth), kcap)
            first = jnp.where(down >= k * count, k * count, first)
        tri = ((right < down) & (right >= first)).astype(jnp.float32).astype(jnp.bfloat16)

        def table(which, part, source, expert, base):
            routing = flat(source[...]).astype(jnp.float32)
            named = (routing == expert.astype(jnp.float32)) & (lane < self.top)
            used = jnp.sum(named.astype(jnp.float32), axis=1, keepdims=True)
            used = jnp.broadcast_to(used, lane.shape)
            rank = dot_f32(tri, used.astype(jnp.bfloat16))
            slot = rank + (kcap + base * span).astype(jnp.float32)
            hit = (used > 0.5) & (slot == lane.astype(jnp.float32))
            self.tabs[which, part] = hit.astype(jnp.float32).astype(jnp.bfloat16)

        z_rt, y_rt, x_rt = self.near[0], self.up[0], self.by[0]
        table(0, 0, z_rt, net.me, net.y)
        table(0, 1, y_rt, net.me, 1 - net.y)
        table(1, 0, z_rt, net.beside_id, net.y)
        table(1, 1, y_rt, net.beside_id, 1 - net.y)
        table(2, 0, z_rt, net.me, net.x)
        table(2, 1, x_rt, net.me, 1 - net.x)
        table(3, 0, z_rt, net.across_id, net.x)
        table(3, 1, x_rt, net.across_id, 1 - net.x)

    def chosen(self, which, near, far):
        rows = dot_f32(self.tabs[which, 0], flat(near), OUTER) + dot_f32(self.tabs[which, 1], flat(far), OUTER)
        return rows[: 2 * self.span].astype(jnp.bfloat16).reshape(2, self.span, -1)

    def share(self, view):
        self.pending += [self.net.push(view, view, peer) for peer in self.net.mates]

    def first_way(self, t):
        net, cols, send, rows = self.net, self.low[t], self.send0[t], self.rows[t]
        self.side0[t].wait_recv() if t else None
        near, far = self.near[t][:, :, cols], self.up[t][...]
        send[...] = self.chosen(1, near, far)
        self.moved0[t] = net.push(send, rows.at[net.core, net.x, :, :, cols], net.beside)
        rows[net.core, net.x, :, :, cols] = self.chosen(0, near, far)
        self.share(rows.at[net.core, net.x, :, :, cols])

    def second_way(self, t):
        net, cols, send, rows = self.net, self.high, self.send1[t], self.rows[t]
        self.side1[t].wait_recv()
        near, far = self.near[t][:, :, cols], self.by[t][...]
        send[...] = self.chosen(3, near, far)
        self.moved1[t] = net.push(send, rows.at[net.core, :, net.y, :, cols], net.across)
        rows[net.core, :, net.y, :, cols] = self.chosen(2, near, far)
        self.share(rows.at[net.core, :, net.y, :, cols])

    def last(self, t):
        net, rows = self.net, self.rows[t]
        self.moved0[t].wait_recv()
        self.share(rows.at[net.core, 1 - net.x, :, :, self.low[t]])
        if t:
            self.moved1[t].wait_recv()
            self.share(rows.at[net.core, :, 1 - net.y, :, self.high])

    def settle(self):
        arrived(self.pending)
        self.pending = []


def dispatch_kernel(depth, group, top, *refs):
    ins, rows, tabs = refs[:3], refs[3:6], refs[6]
    own_sem, send_sem, recv_sem = refs[21:]
    net = Net(depth, group, send_sem, recv_sem)
    step = Dispatch(net, top, ins, rows, tabs, refs[7:16], refs[16:21], own_sem)
    net.barrier()
    step.start()
    step.push_side(0)
    step.push_side(1)
    step.push_deep(2)
    step.tables()
    step.first_way(0)
    step.first_way(1)
    step.second_way(1)
    step.push_side(2)
    step.last(0)
    step.last(1)
    step.first_way(2)
    step.second_way(2)
    step.last(2)
    step.settle()
    net.finish()


def dispatch_scratch(depth, count, span, width):
    half, bf16 = width // 2, jnp.bfloat16
    dense = [pltpu.VMEM((depth, count, w), bf16) for w in (LANES, width, width) + (LANES, half, half) * 2]
    return dense + [pltpu.VMEM((2, span, w), bf16) for w in (LANES, half, half, half, half)]


def dispatch_copies(depth, group):
    return 3 * (depth - 1) + 6 + 5 + 10 * (group - 1)


def semaphores(copies):
    return [pltpu.SemaphoreType.DMA((copies,)), pltpu.SemaphoreType.DMA((copies,))]


VMEM_SPEC = pl.BlockSpec(memory_space=pltpu.VMEM)
ANY_SPEC = pl.BlockSpec(memory_space=pl.ANY)


def dispatch(experts, group, top, capacity, routing, tokens, cotangent):
    depth = experts // 4
    count, width = tokens.shape
    span = depth * capacity
    bf16 = jnp.bfloat16
    return pl.pallas_call(
        functools.partial(dispatch_kernel, depth, group, top),
        out_shape=[
            jax.ShapeDtypeStruct((group, 2, 2, span, LANES), bf16),
            jax.ShapeDtypeStruct((group, 2, 2, span, width), bf16),
            jax.ShapeDtypeStruct((group, 2, 2, span, width), bf16),
            jax.ShapeDtypeStruct((4, 2, depth * count, LANES), bf16),
        ],
        in_specs=[VMEM_SPEC] * 3,
        out_specs=[VMEM_SPEC] * 4,
        scratch_shapes=dispatch_scratch(depth, count, span, width)
        + [pltpu.SemaphoreType.DMA((3,))]
        + semaphores(dispatch_copies(depth, group)),
        compiler_params=pltpu.CompilerParams(
            collective_id=0, has_side_effects=True, vmem_limit_bytes=VMEM_LIMIT
        ),
    )(routing, tokens, cotangent)


JOBS = ((0, 0), (1, 0), (1, 1), (2, 0), (2, 1))


class Job:
    def __init__(self, net, depth, group, tabs, part, out, kind, bufs):
        self.net, self.depth, self.group, self.tabs = net, depth, group, tabs
        self.part, self.out, self.kind = part, out, kind
        (self.mate, self.give, self.own, self.take, self.far, self.near, self.came, self.deep) = bufs
        width = self.give.shape[-1]
        self.cols, self.every = pl.ds(kind * width, width), pl.ds(0, width)
        self.first, self.second = (net.beside, net.across) if kind == 0 else (net.across, net.beside)

    def pick(self, ref, lead, remote, cols):
        net = self.net
        if self.kind == 0:
            return ref.at[lead, 1 - net.x if remote else net.x, :, :, cols]
        return ref.at[lead, :, 1 - net.y if remote else net.y, :, cols]

    def exchange(self):
        net, group = self.net, self.group
        self.copies0 = []
        for remote in (True, False):
            self.copies0.append([
                net.push(
                    self.pick(self.part, (net.core + k) % group, remote, self.cols),
                    self.pick(self.mate, k - 1, remote, self.every),
                    net.mates[k - 1],
                )
                for k in range(1, group)
            ])

    def total(self, remote):
        acc = self.pick(self.part, self.net.core, remote, self.cols)[...].astype(jnp.float32)
        for k in range(1, self.group):
            acc = acc + self.pick(self.mate, k - 1, remote, self.every)[...].astype(jnp.float32)
        return acc.astype(jnp.bfloat16)

    def hop1(self):
        arrived(self.copies0[0])
        self.give[...] = self.total(True)
        self.copy1 = self.net.push(self.give, self.take, self.first)

    def keep(self):
        arrived(self.copies0[1])
        self.own[...] = self.total(False)

    def spread(self, part):
        rows, which = 2 * self.give.shape[1], 2 * self.kind
        mine = dot_f32(self.tabs[which, part, :, :rows], flat(self.own[...]))
        theirs = dot_f32(self.tabs[which + 1, part, :, :rows], flat(self.take[...]))
        return (mine + theirs).astype(jnp.bfloat16).reshape(self.far.shape)

    def hop2(self):
        self.copy1.wait_recv()
        self.far[...] = self.spread(1)
        self.copy2 = self.net.push(self.far, self.came, self.second)
        self.near[...] = self.spread(0)

    def hop3(self):
        net, depth = self.net, self.depth
        self.copy2.wait_recv()
        self.near[...] = (self.near[...].astype(jnp.float32) + self.came[...].astype(jnp.float32)).astype(jnp.bfloat16)
        self.copies3 = [
            net.push(self.near.at[(net.z + k) % depth], self.deep.at[net.z], net.deep[k - 1]) for k in range(1, depth)
        ]

    def sum(self):
        z, depth = self.net.z, self.depth
        arrived(self.copies3)
        acc = self.near[z].astype(jnp.float32)
        for k in range(1, depth):
            acc = acc + self.deep[(z + k) % depth].astype(jnp.float32)
        return acc

    def home(self):
        self.out[:, self.cols] = self.sum().astype(self.out.dtype)


def jobs_scratch(depth, group, count, span, width):
    bf16, half, bufs = jnp.bfloat16, width // 2, []
    for source, kind in JOBS:
        w = LANES if source == 0 else half
        bufs += [pltpu.VMEM((max(1, group - 1), 2, 2, span, w), bf16)]
        bufs += [pltpu.VMEM((2, span, w), bf16)] * 3
        bufs += [pltpu.VMEM((depth, count, w), bf16)] * 4
    return bufs


def jobs_copies(depth, group):
    return len(JOBS) * (2 * (group - 1) + 2 + depth - 1)


def make_jobs(net, depth, group, tabs, parts, outs, bufs):
    return [
        Job(net, depth, group, tabs, parts[source], outs[source], kind, bufs[8 * i : 8 * i + 8])
        for i, (source, kind) in enumerate(JOBS)
    ]


def combine_kernel(depth, group, *refs):
    tabs, parts, outs = refs[0], refs[1:4], refs[4:7]
    net = Net(depth, group, refs[-2], refs[-1])
    net.barrier()
    jobs = make_jobs(net, depth, group, tabs, parts, outs, refs[7:-2])
    for name in ("exchange", "hop1", "keep", "hop2", "hop3", "home"):
        for job in jobs:
            getattr(job, name)()
    net.finish()


def combine(experts, group, capacity, count, tabs, parts):
    depth = experts // 4
    width = parts[1].shape[-1]
    bf16 = jnp.bfloat16
    return pl.pallas_call(
        functools.partial(combine_kernel, depth, group),
        out_shape=[
            jax.ShapeDtypeStruct((count, LANES), jnp.float32),
            jax.ShapeDtypeStruct((count, width), bf16),
            jax.ShapeDtypeStruct((count, width), bf16),
        ],
        in_specs=[VMEM_SPEC] * 4,
        out_specs=[VMEM_SPEC] * 3,
        scratch_shapes=jobs_scratch(depth, group, count, depth * capacity, width)
        + semaphores(jobs_copies(depth, group)),
        compiler_params=pltpu.CompilerParams(
            collective_id=1, has_side_effects=True, vmem_limit_bytes=VMEM_LIMIT
        ),
    )(tabs, *parts)


def layer_kernel(depth, group, top, *refs):
    ins, (wg_hbm, wu_hbm, wd_hbm) = refs[:3], refs[3:6]
    (mixed, token_grad, gate_grad, row_tok, row_back, hid_t, pre_t, upv_t) = refs[6:14]
    (wg, wu, wd, row_rt, row_cot, tabs, row_gate, gp, up, bh, hid, pre, upv, ext_part, out_part, back_part, acc, gate_cols) = refs[14:32]
    dense, routed = refs[32:41], refs[41:46]
    weight_sem, own_sem, send_sem, recv_sem = refs[-4:]
    bufs = refs[46:-4]
    net = Net(depth, group, send_sem, recv_sem)
    step = Dispatch(net, top, ins, (row_rt, row_tok, row_cot), tabs, dense, routed, own_sem)
    jobs = make_jobs(net, depth, group, tabs, (ext_part, out_part, back_part), (gate_cols, mixed, token_grad), bufs)
    forward, back = jobs[:3], jobs[3:]
    slots, ff, width = gp.shape[0], wg.shape[0], wg.shape[1]
    lead = row_tok.shape[:4]
    chunk = 512
    net.barrier()
    weights = []
    for i, (src, dst) in enumerate(((wg_hbm, wg), (wu_hbm, wu), (wd_hbm, wd))):
        copy = pltpu.make_async_copy(src.at[0], dst, weight_sem.at[i])
        weights.append(copy)

    step.start()
    for copy in weights:
        copy.start()
    step.push_side(0)
    step.push_side(1)
    step.push_deep(2)
    step.tables()
    step.first_way(0)
    step.first_way(1)
    step.second_way(1)
    step.push_side(2)
    step.last(0)
    step.last(1)
    step.settle()

    lane = lax.broadcasted_iota(jnp.int32, (slots, LANES), 1)
    routing = row_rt[...].reshape(slots, LANES).astype(jnp.float32)
    gates = pltpu.roll(routing, LANES - top, 1)
    named = (routing == net.me.astype(jnp.float32)) & (lane < top)
    row_gate[...] = jnp.broadcast_to(jnp.sum(jnp.where(named, gates, 0.0), axis=1, keepdims=True), (slots, LANES))

    for copy in weights:
        copy.wait()
    gp[...] = dot_f32(row_tok[...].reshape(slots, width), wg[...], INNER)
    step.first_way(2)
    step.second_way(2)
    up[...] = dot_f32(row_tok[...].reshape(slots, width), wu[...], INNER)
    step.last(2)

    rows = 16

    @pl.loop(0, slots // rows)
    def _(i):
        at = pl.ds(pl.multiple_of(i * rows, rows), rows)
        g = gp[at, :]
        hid[at, pl.ds(0, ff)] = (g * jax.nn.sigmoid(g) * up[at, :]).astype(jnp.bfloat16)

    step.settle()
    acc[...] = jnp.zeros_like(acc)

    @pl.loop(0, width // chunk)
    def _(i):
        cols = pl.ds(pl.multiple_of(i * chunk, chunk), chunk)
        value = dot_f32(hid[:, :ff], wd[:, cols])
        cot = row_cot[:, :, :, :, cols].reshape(slots, chunk).astype(jnp.float32)
        product = value * cot
        for j in range(chunk // LANES):
            acc[...] += product[:, j * LANES : (j + 1) * LANES]
        gate = row_gate[:, :1]
        out_part[:, :, :, :, cols] = (value * gate).astype(jnp.bfloat16).reshape(lead + (chunk,))
        row_back[:, :, :, :, cols] = (cot * gate).astype(jnp.bfloat16).reshape(lead + (chunk,))

    row_grad = jnp.sum(acc[...], axis=1, keepdims=True)
    row_high = row_grad.astype(jnp.bfloat16).astype(jnp.float32)
    row_low = row_grad - row_high
    ext = jnp.where(lane == net.me, row_high, jnp.where(lane == LANES // 2 + net.me, row_low, 0.0))
    ext_part[...] = ext.astype(jnp.bfloat16).reshape(ext_part.shape)
    for job in forward:
        job.exchange()
    bh[...] = dot_f32(row_back[...].reshape(slots, width), wd[...], INNER)
    for name in ("hop1", "keep"):
        for job in forward:
            getattr(job, name)()

    @pl.loop(0, slots // rows)
    def _(i):
        at = pl.ds(pl.multiple_of(i * rows, rows), rows)
        g, b = gp[at, :], bh[at, :]
        s = jax.nn.sigmoid(g)
        pre[at, pl.ds(0, ff)] = (b * up[at, :] * s * (1.0 + g * (1.0 - s))).astype(jnp.bfloat16)
        upv[at, pl.ds(0, ff)] = (b * g * s).astype(jnp.bfloat16)

    def back_cols(first, last):
        @pl.loop(first, last)
        def _(i):
            cols = pl.ds(pl.multiple_of(i * chunk, chunk), chunk)
            value = dot_f32(pre[:, :ff], wg[:, cols]) + dot_f32(upv[:, :ff], wu[:, cols])
            back_part[:, :, :, :, cols] = value.astype(jnp.bfloat16).reshape(lead + (chunk,))

    for job in forward:
        job.hop2()
    middle = width // chunk // 2
    back_cols(0, middle)
    back[0].exchange()
    back_cols(middle, 2 * middle)
    back[1].exchange()
    for job in forward:
        job.hop3()
    for job in back:
        job.hop1()
    for job in back:
        job.keep()
    for src, dst in ((hid, hid_t), (pre, pre_t), (upv, upv_t)):
        dst[...] = src[...].T[:ff]
    for job in back:
        job.hop2()
    for job in back:
        job.hop3()
    for job in forward:
        job.home()
    count = gate_cols.shape[0]
    lane = lax.broadcasted_iota(jnp.int32, (count, LANES), 1)
    cols = gate_cols[...] + pltpu.roll(gate_cols[...], LANES // 2, 1)
    routing = dense[0][net.z].astype(jnp.float32)
    grads = jnp.zeros((count, LANES), jnp.float32)
    for k in range(top):
        hit = (routing[:, k : k + 1] == lane.astype(jnp.float32)) & (lane < LANES // 2)
        grads = jnp.where(lane == k, jnp.sum(jnp.where(hit, cols, 0.0), axis=1, keepdims=True), grads)
    gate_grad[...] = grads
    for job in back:
        job.home()
    net.finish()


def layer(experts, group, top, capacity, routing, tokens, cotangent, w_gate, w_up, w_down):
    depth = experts // 4
    count, width = tokens.shape
    ff = w_gate.shape[1]
    span = depth * capacity
    slots = group * 4 * span
    wide = -(-ff // LANES) * LANES
    bf16, f32 = jnp.bfloat16, jnp.float32
    blocks = (group, 2, 2, span)
    scratch = [
        pltpu.VMEM((ff, width), bf16), pltpu.VMEM((ff, width), bf16), pltpu.VMEM((ff, width), bf16),
        pltpu.VMEM(blocks + (LANES,), bf16), pltpu.VMEM(blocks + (width,), bf16),
        pltpu.VMEM((4, 2, depth * count, LANES), bf16), pltpu.VMEM((slots, LANES), f32),
        pltpu.VMEM((slots, ff), f32), pltpu.VMEM((slots, ff), f32), pltpu.VMEM((slots, ff), f32),
        pltpu.VMEM((slots, wide), bf16), pltpu.VMEM((slots, wide), bf16), pltpu.VMEM((slots, wide), bf16),
        pltpu.VMEM(blocks + (LANES,), bf16), pltpu.VMEM(blocks + (width,), bf16), pltpu.VMEM(blocks + (width,), bf16),
        pltpu.VMEM((slots, LANES), f32), pltpu.VMEM((count, LANES), f32),
    ]
    copies = dispatch_copies(depth, group) + jobs_copies(depth, group)
    return pl.pallas_call(
        functools.partial(layer_kernel, depth, group, top),
        out_shape=[
            jax.ShapeDtypeStruct((count, width), bf16),
            jax.ShapeDtypeStruct((count, width), bf16),
            jax.ShapeDtypeStruct((count, LANES), f32),
            jax.ShapeDtypeStruct(blocks + (width,), bf16),
            jax.ShapeDtypeStruct(blocks + (width,), bf16),
        ] + [jax.ShapeDtypeStruct((ff, slots), bf16)] * 3,
        in_specs=[ANY_SPEC] * 6,
        out_specs=[VMEM_SPEC] * 8,
        scratch_shapes=scratch
        + dispatch_scratch(depth, count, span, width)
        + jobs_scratch(depth, group, count, span, width)
        + [pltpu.SemaphoreType.DMA((3,)), pltpu.SemaphoreType.DMA((3,))]
        + semaphores(copies),
        compiler_params=pltpu.CompilerParams(
            collective_id=2, has_side_effects=True, vmem_limit_bytes=VMEM_LIMIT
        ),
    )(routing, tokens, cotangent, w_gate, w_up, w_down)


def per_device(tokens, cotangent, route_gates, routes, w_gate, w_up, w_down):
    experts, group = lax.axis_size("expert"), lax.axis_size("dp")
    token_count, top_count = routes.shape
    width = tokens.shape[1]
    capacity = max(2, token_count * top_count * 4 // (3 * experts))
    slots = experts * group * capacity
    gate_shard, up_shard, down_shard = (w_gate[0], w_up[0], w_down[0])
    me = lax.axis_index("expert")

    routing = jnp.concatenate([routes.astype(jnp.bfloat16), route_gates], axis=1)
    routing = jnp.pad(routing, ((0, 0), (0, LANES - 2 * top_count)))
    if 2 * slots * width * tokens.dtype.itemsize <= FUSED_LIMIT:
        mixed, token_grad, gate_grad, rows_in, rows_back, hid_t, pre_t, upv_t = layer(
            experts, group, top_count, capacity, routing, tokens, cotangent, w_gate, w_up, w_down
        )
        rows_in, rows_back = rows_in.reshape(slots, width), rows_back.reshape(slots, width)
        grad_down = dot_f32(hid_t, rows_back)
        grad_gate = dot_f32(pre_t, rows_in)
        grad_up = dot_f32(upv_t, rows_in)
        return (mixed, token_grad, gate_grad[:, :top_count], grad_gate[None], grad_up[None], grad_down[None])
    row_rt, row_tok, row_cot, tabs = dispatch(experts, group, top_count, capacity, routing, tokens, cotangent)
    shape = row_tok.shape
    row_rt = row_rt.reshape(slots, LANES).astype(jnp.float32)
    rows_in, rows_cot = row_tok.reshape(slots, width), row_cot.reshape(slots, width)
    named = row_rt[:, :top_count] == me.astype(jnp.float32)
    row_gate = jnp.sum(jnp.where(named, row_rt[:, top_count : 2 * top_count], 0.0), axis=1)[:, None]

    gate_pre = dot_f32(rows_in, gate_shard, INNER)
    up_pre = dot_f32(rows_in, up_shard, INNER)
    sig = jax.nn.sigmoid(gate_pre)
    hidden = (gate_pre * sig * up_pre).astype(jnp.bfloat16)
    out_rows = dot_f32(hidden, down_shard)
    row_grad = jnp.sum(out_rows * rows_cot.astype(jnp.float32), axis=1)[:, None]
    out_part = (out_rows * row_gate).astype(jnp.bfloat16)
    lane = jnp.arange(LANES, dtype=jnp.int32)[None, :]
    row_high = row_grad.astype(jnp.bfloat16)
    row_low = (row_grad - row_high.astype(jnp.float32)).astype(jnp.bfloat16)
    zero = jnp.zeros((), jnp.bfloat16)
    grad_cols = jnp.where(lane == me, row_high, jnp.where(lane == LANES // 2 + me, row_low, zero))
    rows_back = (rows_cot.astype(jnp.float32) * row_gate).astype(jnp.bfloat16)
    back_hidden = dot_f32(rows_back, down_shard, INNER)
    grad_pre = (back_hidden * up_pre * sig * (1.0 + gate_pre * (1.0 - sig))).astype(jnp.bfloat16)
    grad_upv = (back_hidden * gate_pre * sig).astype(jnp.bfloat16)
    back_part = (dot_f32(grad_pre, gate_shard) + dot_f32(grad_upv, up_shard)).astype(jnp.bfloat16)
    gate_cols, mixed, token_grad = combine(
        experts, group, capacity, token_count, tabs,
        [grad_cols.reshape(shape[:4] + (LANES,)), out_part.reshape(shape), back_part.reshape(shape)],
    )
    grad_down = dot_f32(hidden, rows_back, OUTER)
    grad_gate = dot_f32(grad_pre, rows_in, OUTER)
    grad_up = dot_f32(grad_upv, rows_in, OUTER)
    column = lane[:, None, :] % (LANES // 2)
    gate_grad = jnp.sum(jnp.where(routes[:, :, None] == column, gate_cols[:, None, :], 0.0), axis=2)
    return (mixed, token_grad, gate_grad, grad_gate[None], grad_up[None], grad_down[None])


def solution(mesh):
    row = P(("expert", "dp"), None)
    wide = P("expert", "dp", None)
    return jax.shard_map(
        per_device,
        mesh=mesh,
        in_specs=(row, row, row, row, wide, wide, wide),
        out_specs=(row, row, row, wide, wide, wide),
        check_vma=False,
    )
```

```python
import functools

import jax
import jax.numpy as jnp
from jax import lax
from jax.experimental import pallas as pl
from jax.experimental.pallas import tpu as pltpu
from jax.sharding import PartitionSpec as P

INNER = (((1,), (1,)), ((), ()))
OUTER = (((0,), (0,)), ((), ()))
LANES = 128
VMEM_LIMIT = 60 * 1024 * 1024
FUSED_LIMIT = 4 * 1024 * 1024


def dot_f32(left, right, dims=(((1,), (0,)), ((), ()))):
    return lax.dot_general(left, right, dims, preferred_element_type=jnp.float32)


class Net:
    def __init__(self, depth, group, send_sem, recv_sem):
        me, core = lax.axis_index("expert"), lax.axis_index("dp")
        z, y, x = me // 4, (me // 2) % 2, me % 2
        self.me, self.core, self.z, self.y, self.x = me, core, z, y, x

        def at(zz, yy, xx, cc):
            return (zz * 4 + yy * 2 + xx, cc)

        self.deep = [at((z + k) % depth, y, x, core) for k in range(1, depth)]
        self.across, self.beside = at(z, 1 - y, x, core), at(z, y, 1 - x, core)
        self.mates = [at(z, y, x, (core + k) % group) for k in range(1, group)]
        self.across_id, self.beside_id = self.across[0], self.beside[0]
        self.send_sem, self.recv_sem = send_sem, recv_sem
        self.sent, self.used = [], 0

    def barrier(self):
        peers = self.deep + [self.across, self.beside] + self.mates
        barrier = pltpu.get_barrier_semaphore()
        for peer in peers:
            pl.semaphore_signal(barrier, inc=1, device_id=peer, device_id_type=pl.DeviceIdType.MESH)
        pl.semaphore_wait(barrier, len(peers))

    def push(self, src, dst, peer):
        index = self.used
        self.used += 1
        copy = pltpu.make_async_remote_copy(
            src_ref=src, dst_ref=dst, send_sem=self.send_sem.at[index], recv_sem=self.recv_sem.at[index],
            device_id=peer, device_id_type=pl.DeviceIdType.MESH,
        )
        copy.start()
        self.sent.append(copy)
        return copy

    def finish(self):
        for copy in self.sent:
            copy.wait_send()


def arrived(copies):
    for copy in copies:
        copy.wait_recv()


def flat(value):
    return value.reshape(-1, value.shape[-1])


class Dispatch:
    def __init__(self, net, top, ins, rows, tabs, dense, routed, own_sem):
        self.net, self.top, self.ins, self.rows, self.tabs = net, top, ins, rows, tabs
        self.near, self.up, self.by = dense[:3], dense[3:6], dense[6:9]
        self.send0, self.send1 = (routed[0], routed[1], routed[2]), (None, routed[3], routed[4])
        self.own_sem = own_sem
        half = ins[1].shape[1] // 2
        self.low = (pl.ds(0, LANES), pl.ds(0, half), pl.ds(0, half))
        self.high = pl.ds(half, half)
        self.span = rows[0].shape[3]
        self.pending = []
        self.moved0, self.moved1, self.deep, self.side0, self.side1 = {}, {}, {}, {}, {}

    def start(self):
        net = self.net
        own = []
        for t in range(3):
            copy = pltpu.make_async_copy(self.ins[t], self.near[t].at[net.z], self.own_sem.at[t])
            copy.start()
            own.append(copy)
        self.push_deep(0)
        self.push_deep(1)
        for copy in own:
            copy.wait()

    def push_deep(self, t):
        net = self.net
        self.deep[t] = [net.push(self.ins[t], self.near[t].at[net.z], peer) for peer in net.deep]

    def push_side(self, t):
        net = self.net
        arrived(self.deep[t])
        if t == 0:
            self.side0[t] = net.push(self.near[t], self.up[t], net.across)
            self.side1[t] = net.push(self.near[t], self.by[t], net.beside)
        else:
            self.side0[t] = net.push(self.near[t].at[:, :, self.low[t]], self.up[t], net.across)
            self.side1[t] = net.push(self.near[t].at[:, :, self.high], self.by[t], net.beside)

    def tables(self):
        net, span, count = self.net, self.span, self.ins[0].shape[0]
        self.side0[0].wait_recv()
        self.side1[0].wait_recv()
        depth = self.near[0].shape[0]
        total = depth * count
        lane = lax.broadcasted_iota(jnp.int32, (total, LANES), 1)
        row = lax.broadcasted_iota(jnp.int32, (total, LANES), 0)
        down, right = lax.broadcasted_iota(jnp.int32, (total, total), 0), lax.broadcasted_iota(jnp.int32, (total, total), 1)
        kcap = jnp.zeros((total, LANES), jnp.int32)
        first = jnp.zeros((total, total), jnp.int32)
        for k in range(1, depth):
            kcap = jnp.where(row >= k * count, k * (span // depth), kcap)
            first = jnp.where(down >= k * count, k * count, first)
        tri = ((right < down) & (right >= first)).astype(jnp.float32).astype(jnp.bfloat16)

        def table(which, part, source, expert, base):
            routing = flat(source[...]).astype(jnp.float32)
            named = (routing == expert.astype(jnp.float32)) & (lane < self.top)
            used = jnp.sum(named.astype(jnp.float32), axis=1, keepdims=True)
            used = jnp.broadcast_to(used, lane.shape)
            rank = dot_f32(tri, used.astype(jnp.bfloat16))
            slot = rank + (kcap + base * span).astype(jnp.float32)
            hit = (used > 0.5) & (slot == lane.astype(jnp.float32))
            self.tabs[which, part] = hit.astype(jnp.float32).astype(jnp.bfloat16)

        z_rt, y_rt, x_rt = self.near[0], self.up[0], self.by[0]
        table(0, 0, z_rt, net.me, net.y)
        table(0, 1, y_rt, net.me, 1 - net.y)
        table(1, 0, z_rt, net.beside_id, net.y)
        table(1, 1, y_rt, net.beside_id, 1 - net.y)
        table(2, 0, z_rt, net.me, net.x)
        table(2, 1, x_rt, net.me, 1 - net.x)
        table(3, 0, z_rt, net.across_id, net.x)
        table(3, 1, x_rt, net.across_id, 1 - net.x)

    def chosen(self, which, near, far):
        rows = dot_f32(self.tabs[which, 0], flat(near), OUTER) + dot_f32(self.tabs[which, 1], flat(far), OUTER)
        return rows[: 2 * self.span].astype(jnp.bfloat16).reshape(2, self.span, -1)

    def share(self, view):
        self.pending += [self.net.push(view, view, peer) for peer in self.net.mates]

    def first_way(self, t):
        net, cols, send, rows = self.net, self.low[t], self.send0[t], self.rows[t]
        self.side0[t].wait_recv() if t else None
        near, far = self.near[t][:, :, cols], self.up[t][...]
        send[...] = self.chosen(1, near, far)
        self.moved0[t] = net.push(send, rows.at[net.core, net.x, :, :, cols], net.beside)
        rows[net.core, net.x, :, :, cols] = self.chosen(0, near, far)
        self.share(rows.at[net.core, net.x, :, :, cols])

    def second_way(self, t):
        net, cols, send, rows = self.net, self.high, self.send1[t], self.rows[t]
        self.side1[t].wait_recv()
        near, far = self.near[t][:, :, cols], self.by[t][...]
        send[...] = self.chosen(3, near, far)
        self.moved1[t] = net.push(send, rows.at[net.core, :, net.y, :, cols], net.across)
        rows[net.core, :, net.y, :, cols] = self.chosen(2, near, far)
        self.share(rows.at[net.core, :, net.y, :, cols])

    def last(self, t):
        net, rows = self.net, self.rows[t]
        self.moved0[t].wait_recv()
        self.share(rows.at[net.core, 1 - net.x, :, :, self.low[t]])
        if t:
            self.moved1[t].wait_recv()
            self.share(rows.at[net.core, :, 1 - net.y, :, self.high])

    def settle(self):
        arrived(self.pending)
        self.pending = []


def dispatch_kernel(depth, group, top, *refs):
    ins, rows, tabs = refs[:3], refs[3:6], refs[6]
    own_sem, send_sem, recv_sem = refs[21:]
    net = Net(depth, group, send_sem, recv_sem)
    step = Dispatch(net, top, ins, rows, tabs, refs[7:16], refs[16:21], own_sem)
    net.barrier()
    step.start()
    step.push_side(0)
    step.push_side(1)
    step.push_deep(2)
    step.tables()
    step.first_way(0)
    step.first_way(1)
    step.second_way(1)
    step.push_side(2)
    step.last(0)
    step.last(1)
    step.first_way(2)
    step.second_way(2)
    step.last(2)
    step.settle()
    net.finish()


def dispatch_scratch(depth, count, span, width):
    half, bf16 = width // 2, jnp.bfloat16
    dense = [pltpu.VMEM((depth, count, w), bf16) for w in (LANES, width, width) + (LANES, half, half) * 2]
    return dense + [pltpu.VMEM((2, span, w), bf16) for w in (LANES, half, half, half, half)]


def dispatch_copies(depth, group):
    return 3 * (depth - 1) + 6 + 5 + 10 * (group - 1)


def semaphores(copies):
    return [pltpu.SemaphoreType.DMA((copies,)), pltpu.SemaphoreType.DMA((copies,))]


VMEM_SPEC = pl.BlockSpec(memory_space=pltpu.VMEM)
ANY_SPEC = pl.BlockSpec(memory_space=pl.ANY)


def dispatch(experts, group, top, capacity, routing, tokens, cotangent):
    depth = experts // 4
    count, width = tokens.shape
    span = depth * capacity
    bf16 = jnp.bfloat16
    return pl.pallas_call(
        functools.partial(dispatch_kernel, depth, group, top),
        out_shape=[
            jax.ShapeDtypeStruct((group, 2, 2, span, LANES), bf16),
            jax.ShapeDtypeStruct((group, 2, 2, span, width), bf16),
            jax.ShapeDtypeStruct((group, 2, 2, span, width), bf16),
            jax.ShapeDtypeStruct((4, 2, depth * count, LANES), bf16),
        ],
        in_specs=[VMEM_SPEC] * 3,
        out_specs=[VMEM_SPEC] * 4,
        scratch_shapes=dispatch_scratch(depth, count, span, width)
        + [pltpu.SemaphoreType.DMA((3,))]
        + semaphores(dispatch_copies(depth, group)),
        compiler_params=pltpu.CompilerParams(
            collective_id=0, has_side_effects=True, vmem_limit_bytes=VMEM_LIMIT
        ),
    )(routing, tokens, cotangent)


JOBS = ((0, 0), (1, 0), (1, 1), (2, 0), (2, 1))


class Job:
    def __init__(self, net, depth, group, tabs, part, out, kind, bufs):
        self.net, self.depth, self.group, self.tabs = net, depth, group, tabs
        self.part, self.out, self.kind = part, out, kind
        (self.mate, self.give, self.own, self.take, self.far, self.near, self.came, self.deep) = bufs
        width = self.give.shape[-1]
        self.cols, self.every = pl.ds(kind * width, width), pl.ds(0, width)
        self.first, self.second = (net.beside, net.across) if kind == 0 else (net.across, net.beside)

    def pick(self, ref, lead, remote, cols):
        net = self.net
        if self.kind == 0:
            return ref.at[lead, 1 - net.x if remote else net.x, :, :, cols]
        return ref.at[lead, :, 1 - net.y if remote else net.y, :, cols]

    def exchange(self):
        net, group = self.net, self.group
        self.copies0 = []
        for remote in (True, False):
            self.copies0.append([
                net.push(
                    self.pick(self.part, (net.core + k) % group, remote, self.cols),
                    self.pick(self.mate, k - 1, remote, self.every),
                    net.mates[k - 1],
                )
                for k in range(1, group)
            ])

    def total(self, remote):
        acc = self.pick(self.part, self.net.core, remote, self.cols)[...].astype(jnp.float32)
        for k in range(1, self.group):
            acc = acc + self.pick(self.mate, k - 1, remote, self.every)[...].astype(jnp.float32)
        return acc.astype(jnp.bfloat16)

    def hop1(self):
        arrived(self.copies0[0])
        self.give[...] = self.total(True)
        self.copy1 = self.net.push(self.give, self.take, self.first)

    def keep(self):
        arrived(self.copies0[1])
        self.own[...] = self.total(False)

    def spread(self, part):
        rows, which = 2 * self.give.shape[1], 2 * self.kind
        mine = dot_f32(self.tabs[which, part, :, :rows], flat(self.own[...]))
        theirs = dot_f32(self.tabs[which + 1, part, :, :rows], flat(self.take[...]))
        return (mine + theirs).astype(jnp.bfloat16).reshape(self.far.shape)

    def hop2(self):
        self.copy1.wait_recv()
        self.far[...] = self.spread(1)
        self.copy2 = self.net.push(self.far, self.came, self.second)
        self.near[...] = self.spread(0)

    def hop3(self):
        net, depth = self.net, self.depth
        self.copy2.wait_recv()
        self.near[...] = (self.near[...].astype(jnp.float32) + self.came[...].astype(jnp.float32)).astype(jnp.bfloat16)
        self.copies3 = [
            net.push(self.near.at[(net.z + k) % depth], self.deep.at[net.z], net.deep[k - 1]) for k in range(1, depth)
        ]

    def sum(self):
        z, depth = self.net.z, self.depth
        arrived(self.copies3)
        acc = self.near[z].astype(jnp.float32)
        for k in range(1, depth):
            acc = acc + self.deep[(z + k) % depth].astype(jnp.float32)
        return acc

    def home(self):
        self.out[:, self.cols] = self.sum().astype(self.out.dtype)


def jobs_scratch(depth, group, count, span, width):
    bf16, half, bufs = jnp.bfloat16, width // 2, []
    for source, kind in JOBS:
        w = LANES if source == 0 else half
        bufs += [pltpu.VMEM((max(1, group - 1), 2, 2, span, w), bf16)]
        bufs += [pltpu.VMEM((2, span, w), bf16)] * 3
        bufs += [pltpu.VMEM((depth, count, w), bf16)] * 4
    return bufs


def jobs_copies(depth, group):
    return len(JOBS) * (2 * (group - 1) + 2 + depth - 1)


def make_jobs(net, depth, group, tabs, parts, outs, bufs):
    return [
        Job(net, depth, group, tabs, parts[source], outs[source], kind, bufs[8 * i : 8 * i + 8])
        for i, (source, kind) in enumerate(JOBS)
    ]


def combine_kernel(depth, group, *refs):
    tabs, parts, outs = refs[0], refs[1:4], refs[4:7]
    net = Net(depth, group, refs[-2], refs[-1])
    net.barrier()
    jobs = make_jobs(net, depth, group, tabs, parts, outs, refs[7:-2])
    for name in ("exchange", "hop1", "keep", "hop2", "hop3", "home"):
        for job in jobs:
            getattr(job, name)()
    net.finish()


def combine(experts, group, capacity, count, tabs, parts):
    depth = experts // 4
    width = parts[1].shape[-1]
    bf16 = jnp.bfloat16
    return pl.pallas_call(
        functools.partial(combine_kernel, depth, group),
        out_shape=[
            jax.ShapeDtypeStruct((count, LANES), jnp.float32),
            jax.ShapeDtypeStruct((count, width), bf16),
            jax.ShapeDtypeStruct((count, width), bf16),
        ],
        in_specs=[VMEM_SPEC] * 4,
        out_specs=[VMEM_SPEC] * 3,
        scratch_shapes=jobs_scratch(depth, group, count, depth * capacity, width)
        + semaphores(jobs_copies(depth, group)),
        compiler_params=pltpu.CompilerParams(
            collective_id=1, has_side_effects=True, vmem_limit_bytes=VMEM_LIMIT
        ),
    )(tabs, *parts)


def layer_kernel(depth, group, top, *refs):
    (routes, route_gates, tokens, cotangent, wg_hbm, wu_hbm, wd_hbm), refs = refs[:7], refs[1:]
    (mixed, token_grad, gate_grad, row_tok, row_back, hid_t, pre_t, upv_t) = refs[6:14]
    (wg, wu, wd, row_rt, row_cot, tabs, row_gate, gp, up, bh, hid, pre, upv, ext_part, out_part, back_part, acc, gate_cols) = refs[14:32]
    dense, routed = refs[32:41], refs[41:46]
    weight_sem, own_sem, send_sem, recv_sem = refs[-4:]
    rt, square = refs[-6:-4]
    bufs = refs[46:-6]
    ins = (rt, tokens, cotangent)
    net = Net(depth, group, send_sem, recv_sem)
    count = rt.shape[0]
    square[...] = jnp.zeros_like(square)
    square[:top, :count] = routes[...].astype(jnp.float32)
    square[top : 2 * top, :count] = route_gates[...].astype(jnp.float32)
    rt[...] = square[...].T[:count].astype(jnp.bfloat16)
    step = Dispatch(net, top, ins, (row_rt, row_tok, row_cot), tabs, dense, routed, own_sem)
    jobs = make_jobs(net, depth, group, tabs, (ext_part, out_part, back_part), (gate_cols, mixed, token_grad), bufs)
    forward, back = jobs[:3], jobs[3:]
    slots, ff, width = gp.shape[0], wg.shape[0], wg.shape[1]
    lead = row_tok.shape[:4]
    chunk = 512
    net.barrier()
    weights = []
    for i, (src, dst) in enumerate(((wg_hbm, wg), (wu_hbm, wu), (wd_hbm, wd))):
        copy = pltpu.make_async_copy(src.at[0], dst, weight_sem.at[i])
        weights.append(copy)

    step.start()
    for copy in weights:
        copy.start()
    step.push_side(0)
    step.push_side(1)
    step.push_deep(2)
    step.tables()
    step.first_way(0)
    step.first_way(1)
    step.second_way(1)
    step.push_side(2)
    step.last(0)
    step.last(1)
    step.settle()

    lane = lax.broadcasted_iota(jnp.int32, (slots, LANES), 1)
    routing = row_rt[...].reshape(slots, LANES).astype(jnp.float32)
    gates = pltpu.roll(routing, LANES - top, 1)
    named = (routing == net.me.astype(jnp.float32)) & (lane < top)
    row_gate[...] = jnp.broadcast_to(jnp.sum(jnp.where(named, gates, 0.0), axis=1, keepdims=True), (slots, LANES))

    for copy in weights:
        copy.wait()
    gp[...] = dot_f32(row_tok[...].reshape(slots, width), wg[...], INNER)
    step.first_way(2)
    step.second_way(2)
    up[...] = dot_f32(row_tok[...].reshape(slots, width), wu[...], INNER)
    step.last(2)

    rows = 16

    @pl.loop(0, slots // rows)
    def _(i):
        at = pl.ds(pl.multiple_of(i * rows, rows), rows)
        g = gp[at, :]
        hid[at, pl.ds(0, ff)] = (g * jax.nn.sigmoid(g) * up[at, :]).astype(jnp.bfloat16)

    step.settle()
    acc[...] = jnp.zeros_like(acc)

    @pl.loop(0, width // chunk)
    def _(i):
        cols = pl.ds(pl.multiple_of(i * chunk, chunk), chunk)
        value = dot_f32(hid[:, :ff], wd[:, cols])
        cot = row_cot[:, :, :, :, cols].reshape(slots, chunk).astype(jnp.float32)
        product = value * cot
        for j in range(chunk // LANES):
            acc[...] += product[:, j * LANES : (j + 1) * LANES]
        gate = row_gate[:, :1]
        out_part[:, :, :, :, cols] = (value * gate).astype(jnp.bfloat16).reshape(lead + (chunk,))
        row_back[:, :, :, :, cols] = (cot * gate).astype(jnp.bfloat16).reshape(lead + (chunk,))

    row_grad = jnp.sum(acc[...], axis=1, keepdims=True)
    row_high = row_grad.astype(jnp.bfloat16).astype(jnp.float32)
    row_low = row_grad - row_high
    ext = jnp.where(lane == net.me, row_high, jnp.where(lane == LANES // 2 + net.me, row_low, 0.0))
    ext_part[...] = ext.astype(jnp.bfloat16).reshape(ext_part.shape)
    for job in forward:
        job.exchange()
    bh[...] = dot_f32(row_back[...].reshape(slots, width), wd[...], INNER)
    for name in ("hop1", "keep"):
        for job in forward:
            getattr(job, name)()

    @pl.loop(0, slots // rows)
    def _(i):
        at = pl.ds(pl.multiple_of(i * rows, rows), rows)
        g, b = gp[at, :], bh[at, :]
        s = jax.nn.sigmoid(g)
        pre[at, pl.ds(0, ff)] = (b * up[at, :] * s * (1.0 + g * (1.0 - s))).astype(jnp.bfloat16)
        upv[at, pl.ds(0, ff)] = (b * g * s).astype(jnp.bfloat16)

    def back_cols(first, last):
        @pl.loop(first, last)
        def _(i):
            cols = pl.ds(pl.multiple_of(i * chunk, chunk), chunk)
            value = dot_f32(pre[:, :ff], wg[:, cols]) + dot_f32(upv[:, :ff], wu[:, cols])
            back_part[:, :, :, :, cols] = value.astype(jnp.bfloat16).reshape(lead + (chunk,))

    for job in forward:
        job.hop2()
    middle = width // chunk // 2
    back_cols(0, middle)
    back[0].exchange()
    back_cols(middle, 2 * middle)
    back[1].exchange()
    for job in forward:
        job.hop3()
    for job in back:
        job.hop1()
    for job in back:
        job.keep()
    for src, dst in ((hid, hid_t), (pre, pre_t), (upv, upv_t)):
        dst[...] = src[...].T[:ff]
    for job in back:
        job.hop2()
    for job in back:
        job.hop3()
    for job in forward:
        job.home()
    lane = lax.broadcasted_iota(jnp.int32, (count, LANES), 1)
    cols = gate_cols[...] + pltpu.roll(gate_cols[...], LANES // 2, 1)
    routing = rt[...].astype(jnp.float32)
    grads = jnp.zeros((count, LANES), jnp.float32)
    for k in range(top):
        hit = (routing[:, k : k + 1] == lane.astype(jnp.float32)) & (lane < LANES // 2)
        grads = jnp.where(lane == k, jnp.sum(jnp.where(hit, cols, 0.0), axis=1, keepdims=True), grads)
    square[:count, :] = grads
    gate_grad[...] = square[...].T[: gate_grad.shape[0]]
    for job in back:
        job.home()
    net.finish()


def layer(experts, group, top, capacity, routes, route_gates, tokens, cotangent, w_gate, w_up, w_down):
    depth = experts // 4
    count, width = tokens.shape
    ff = w_gate.shape[1]
    span = depth * capacity
    slots = group * 4 * span
    wide = -(-ff // LANES) * LANES
    bf16, f32 = jnp.bfloat16, jnp.float32
    blocks = (group, 2, 2, span)
    scratch = [
        pltpu.VMEM((ff, width), bf16), pltpu.VMEM((ff, width), bf16), pltpu.VMEM((ff, width), bf16),
        pltpu.VMEM(blocks + (LANES,), bf16), pltpu.VMEM(blocks + (width,), bf16),
        pltpu.VMEM((4, 2, depth * count, LANES), bf16), pltpu.VMEM((slots, LANES), f32),
        pltpu.VMEM((slots, ff), f32), pltpu.VMEM((slots, ff), f32), pltpu.VMEM((slots, ff), f32),
        pltpu.VMEM((slots, wide), bf16), pltpu.VMEM((slots, wide), bf16), pltpu.VMEM((slots, wide), bf16),
        pltpu.VMEM(blocks + (LANES,), bf16), pltpu.VMEM(blocks + (width,), bf16), pltpu.VMEM(blocks + (width,), bf16),
        pltpu.VMEM((slots, LANES), f32), pltpu.VMEM((count, LANES), f32),
    ]
    copies = dispatch_copies(depth, group) + jobs_copies(depth, group)
    return pl.pallas_call(
        functools.partial(layer_kernel, depth, group, top),
        out_shape=[
            jax.ShapeDtypeStruct((count, width), bf16),
            jax.ShapeDtypeStruct((count, width), bf16),
            jax.ShapeDtypeStruct((8, LANES), f32),
            jax.ShapeDtypeStruct(blocks + (width,), bf16),
            jax.ShapeDtypeStruct(blocks + (width,), bf16),
        ] + [jax.ShapeDtypeStruct((ff, slots), bf16)] * 3,
        in_specs=[VMEM_SPEC] * 2 + [ANY_SPEC] * 5,
        out_specs=[VMEM_SPEC] * 8,
        scratch_shapes=scratch
        + dispatch_scratch(depth, count, span, width)
        + jobs_scratch(depth, group, count, span, width)
        + [pltpu.VMEM((count, LANES), bf16), pltpu.VMEM((LANES, LANES), f32)]
        + [pltpu.SemaphoreType.DMA((3,)), pltpu.SemaphoreType.DMA((3,))]
        + semaphores(copies),
        compiler_params=pltpu.CompilerParams(
            collective_id=2, has_side_effects=True, vmem_limit_bytes=VMEM_LIMIT
        ),
    )(routes.T, route_gates.T, tokens, cotangent, w_gate, w_up, w_down)


def weight_kernel(hid_t, pre_t, upv_t, rows_in, rows_back, mixed_in, token_in, route_in, down, gate, up, mixed, token_grad, route_grad):
    down[0] = dot_f32(hid_t[...], rows_back[...])
    gate[0] = dot_f32(pre_t[...], rows_in[...])
    up[0] = dot_f32(upv_t[...], rows_in[...])
    mixed[...] = mixed_in[...]
    token_grad[...] = token_in[...]
    route_grad[...] = route_in[: route_grad.shape[0], : route_grad.shape[1]]


def weight_grads(top, hid_t, pre_t, upv_t, rows_in, rows_back, mixed, token_grad, route_grad):
    ff, slots = hid_t.shape
    count, width = mixed.shape
    chunk = 256
    whole = lambda array: pl.BlockSpec(array.shape, lambda i: (0, 0))
    columns = lambda array: pl.BlockSpec((array.shape[0], chunk), lambda i: (0, i))
    wide = pl.BlockSpec((1, ff, chunk), lambda i: (0, 0, i))
    grads = jax.ShapeDtypeStruct((1, ff, width), jnp.float32)
    route = jax.ShapeDtypeStruct((top, count), jnp.float32)
    return pl.pallas_call(
        weight_kernel,
        grid=(width // chunk,),
        out_shape=[grads, grads, grads, mixed, token_grad, route],
        in_specs=[whole(hid_t)] * 3 + [columns(rows_in)] * 2 + [columns(mixed)] * 2 + [whole(route_grad)],
        out_specs=[wide] * 3 + [columns(mixed)] * 2 + [whole(route)],
        cost_estimate=pl.CostEstimate(
            flops=6 * slots * ff * width, bytes_accessed=12 * ff * width, transcendentals=0
        ),
        compiler_params=pltpu.CompilerParams(vmem_limit_bytes=VMEM_LIMIT),
    )(hid_t, pre_t, upv_t, rows_in, rows_back, mixed, token_grad, route_grad)


def per_device(tokens, cotangent, route_gates, routes, w_gate, w_up, w_down):
    experts, group = lax.axis_size("expert"), lax.axis_size("dp")
    token_count, top_count = routes.shape
    width = tokens.shape[1]
    capacity = max(2, token_count * top_count * 4 // (3 * experts))
    slots = experts * group * capacity
    gate_shard, up_shard, down_shard = (w_gate[0], w_up[0], w_down[0])
    me = lax.axis_index("expert")

    if 2 * slots * width * tokens.dtype.itemsize <= FUSED_LIMIT:
        mixed, token_grad, gate_grad, rows_in, rows_back, hid_t, pre_t, upv_t = layer(
            experts, group, top_count, capacity, routes, route_gates, tokens, cotangent, w_gate, w_up, w_down
        )
        rows_in, rows_back = rows_in.reshape(slots, width), rows_back.reshape(slots, width)
        grad_down, grad_gate, grad_up, mixed, token_grad, gate_grad = weight_grads(
            top_count, hid_t, pre_t, upv_t, rows_in, rows_back, mixed, token_grad, gate_grad
        )
        return (mixed, token_grad, gate_grad.T, grad_gate, grad_up, grad_down)
    routing = jnp.concatenate([routes.astype(jnp.bfloat16), route_gates], axis=1)
    routing = jnp.pad(routing, ((0, 0), (0, LANES - 2 * top_count)))
    row_rt, row_tok, row_cot, tabs = dispatch(experts, group, top_count, capacity, routing, tokens, cotangent)
    shape = row_tok.shape
    row_rt = row_rt.reshape(slots, LANES).astype(jnp.float32)
    rows_in, rows_cot = row_tok.reshape(slots, width), row_cot.reshape(slots, width)
    named = row_rt[:, :top_count] == me.astype(jnp.float32)
    row_gate = jnp.sum(jnp.where(named, row_rt[:, top_count : 2 * top_count], 0.0), axis=1)[:, None]

    gate_pre = dot_f32(rows_in, gate_shard, INNER)
    up_pre = dot_f32(rows_in, up_shard, INNER)
    sig = jax.nn.sigmoid(gate_pre)
    hidden = (gate_pre * sig * up_pre).astype(jnp.bfloat16)
    out_rows = dot_f32(hidden, down_shard)
    row_grad = jnp.sum(out_rows * rows_cot.astype(jnp.float32), axis=1)[:, None]
    out_part = (out_rows * row_gate).astype(jnp.bfloat16)
    lane = jnp.arange(LANES, dtype=jnp.int32)[None, :]
    row_high = row_grad.astype(jnp.bfloat16)
    row_low = (row_grad - row_high.astype(jnp.float32)).astype(jnp.bfloat16)
    zero = jnp.zeros((), jnp.bfloat16)
    grad_cols = jnp.where(lane == me, row_high, jnp.where(lane == LANES // 2 + me, row_low, zero))
    rows_back = (rows_cot.astype(jnp.float32) * row_gate).astype(jnp.bfloat16)
    back_hidden = dot_f32(rows_back, down_shard, INNER)
    grad_pre = (back_hidden * up_pre * sig * (1.0 + gate_pre * (1.0 - sig))).astype(jnp.bfloat16)
    grad_upv = (back_hidden * gate_pre * sig).astype(jnp.bfloat16)
    back_part = (dot_f32(grad_pre, gate_shard) + dot_f32(grad_upv, up_shard)).astype(jnp.bfloat16)
    gate_cols, mixed, token_grad = combine(
        experts, group, capacity, token_count, tabs,
        [grad_cols.reshape(shape[:4] + (LANES,)), out_part.reshape(shape), back_part.reshape(shape)],
    )
    grad_down = dot_f32(hidden, rows_back, OUTER)
    grad_gate = dot_f32(grad_pre, rows_in, OUTER)
    grad_up = dot_f32(grad_upv, rows_in, OUTER)
    column = lane[:, None, :] % (LANES // 2)
    gate_grad = jnp.sum(jnp.where(routes[:, :, None] == column, gate_cols[:, None, :], 0.0), axis=2)
    return (mixed, token_grad, gate_grad, grad_gate[None], grad_up[None], grad_down[None])


def solution(mesh):
    row = P(("expert", "dp"), None)
    wide = P("expert", "dp", None)
    return jax.shard_map(
        per_device,
        mesh=mesh,
        in_specs=(row, row, row, row, wide, wide, wide),
        out_specs=(row, row, row, wide, wide, wide),
        check_vma=False,
    )
```

```python
import functools

import jax
import jax.numpy as jnp
from jax import lax
from jax.experimental import pallas as pl
from jax.experimental.pallas import tpu as pltpu
from jax.sharding import PartitionSpec as P

INNER = (((1,), (1,)), ((), ()))
OUTER = (((0,), (0,)), ((), ()))
LANES = 128
VMEM_LIMIT = 60 * 1024 * 1024
FUSED_LIMIT = 4 * 1024 * 1024
PARTS = 4
ORDER = (0, 2, 1, 3)


def dot_f32(left, right, dims=(((1,), (0,)), ((), ()))):
    return lax.dot_general(left, right, dims, preferred_element_type=jnp.float32)


class Net:
    def __init__(self, depth, group, send_sem, recv_sem):
        me, core = lax.axis_index("expert"), lax.axis_index("dp")
        z, y, x = me // 4, (me // 2) % 2, me % 2
        self.me, self.core, self.z, self.y, self.x = me, core, z, y, x

        def at(zz, yy, xx, cc):
            return (zz * 4 + yy * 2 + xx, cc)

        self.deep = [at((z + k) % depth, y, x, core) for k in range(1, depth)]
        self.across, self.beside = at(z, 1 - y, x, core), at(z, y, 1 - x, core)
        self.mates = [at(z, y, x, (core + k) % group) for k in range(1, group)]
        self.across_id, self.beside_id = self.across[0], self.beside[0]
        self.send_sem, self.recv_sem = send_sem, recv_sem
        self.sent, self.used = [], 0

    def barrier(self):
        peers = self.deep + [self.across, self.beside] + self.mates
        barrier = pltpu.get_barrier_semaphore()
        for peer in peers:
            pl.semaphore_signal(barrier, inc=1, device_id=peer, device_id_type=pl.DeviceIdType.MESH)
        pl.semaphore_wait(barrier, len(peers))

    def push(self, src, dst, peer):
        index = self.used
        self.used += 1
        copy = pltpu.make_async_remote_copy(
            src_ref=src, dst_ref=dst, send_sem=self.send_sem.at[index], recv_sem=self.recv_sem.at[index],
            device_id=peer, device_id_type=pl.DeviceIdType.MESH,
        )
        copy.start()
        self.sent.append(copy)
        return copy

    def finish(self):
        for copy in self.sent:
            copy.wait_send()


def arrived(copies):
    for copy in copies:
        copy.wait_recv()


def flat(value):
    return value.reshape(-1, value.shape[-1])


class Dispatch:
    def __init__(self, net, top, ins, rows, tabs, dense, routed, own_sem):
        self.net, self.top, self.ins, self.rows, self.tabs = net, top, ins, rows, tabs
        self.near, self.up, self.by = dense[:3], dense[3:6], dense[6:9]
        self.send0, self.send1 = (routed[0], routed[1], routed[2]), (None, routed[3], routed[4])
        self.own_sem = own_sem
        self.half, self.chunk = ins[1].shape[1] // 2, ins[1].shape[1] // PARTS
        self.span = rows[0].shape[3]
        self.units = [(t, c) for t in (1, 2) for c in ORDER]
        self.pending, self.moved, self.deep, self.side = {}, {}, {}, {}

    def cols(self, unit):
        t, c = unit
        if t == 0:
            return 0, pl.ds(0, LANES), pl.ds(0, LANES)
        kind = int(2 * c >= PARTS)
        return kind, pl.ds(c * self.chunk, self.chunk), pl.ds(c * self.chunk - kind * self.half, self.chunk)

    def start(self):
        net = self.net
        own = []
        for t in range(3):
            copy = pltpu.make_async_copy(self.ins[t], self.near[t].at[net.z], self.own_sem.at[t])
            copy.start()
            own.append(copy)
        for unit in [(0, 0)] + self.units:
            t, (_, wide, _) = unit[0], self.cols(unit)
            self.deep[unit] = [net.push(self.ins[t].at[:, wide], self.near[t].at[net.z, :, wide], peer) for peer in net.deep]
        for copy in own:
            copy.wait()

    def push_side(self, unit):
        net, t = self.net, unit[0]
        kind, wide, thin = self.cols(unit)
        arrived(self.deep[unit])
        if t == 0:
            self.side[unit] = net.push(self.near[t], self.up[t], net.across)
            self.side_by = net.push(self.near[t], self.by[t], net.beside)
        elif kind == 0:
            self.side[unit] = net.push(self.near[t].at[:, :, wide], self.up[t].at[:, :, thin], net.across)
        else:
            self.side[unit] = net.push(self.near[t].at[:, :, wide], self.by[t].at[:, :, thin], net.beside)

    def tables(self):
        net, span, count = self.net, self.span, self.ins[0].shape[0]
        self.side[0, 0].wait_recv()
        self.side_by.wait_recv()
        depth = self.near[0].shape[0]
        total = depth * count
        lane = lax.broadcasted_iota(jnp.int32, (total, LANES), 1)
        row = lax.broadcasted_iota(jnp.int32, (total, LANES), 0)
        down, right = lax.broadcasted_iota(jnp.int32, (total, total), 0), lax.broadcasted_iota(jnp.int32, (total, total), 1)
        kcap = jnp.zeros((total, LANES), jnp.int32)
        first = jnp.zeros((total, total), jnp.int32)
        for k in range(1, depth):
            kcap = jnp.where(row >= k * count, k * (span // depth), kcap)
            first = jnp.where(down >= k * count, k * count, first)
        tri = ((right < down) & (right >= first)).astype(jnp.float32).astype(jnp.bfloat16)

        def table(which, part, source, expert, base):
            routing = flat(source[...]).astype(jnp.float32)
            named = (routing == expert.astype(jnp.float32)) & (lane < self.top)
            used = jnp.sum(named.astype(jnp.float32), axis=1, keepdims=True)
            used = jnp.broadcast_to(used, lane.shape)
            rank = dot_f32(tri, used.astype(jnp.bfloat16))
            slot = rank + (kcap + base * span).astype(jnp.float32)
            hit = (used > 0.5) & (slot == lane.astype(jnp.float32))
            self.tabs[which, part] = hit.astype(jnp.float32).astype(jnp.bfloat16)

        z_rt, y_rt, x_rt = self.near[0], self.up[0], self.by[0]
        table(0, 0, z_rt, net.me, net.y)
        table(0, 1, y_rt, net.me, 1 - net.y)
        table(1, 0, z_rt, net.beside_id, net.y)
        table(1, 1, y_rt, net.beside_id, 1 - net.y)
        table(2, 0, z_rt, net.me, net.x)
        table(2, 1, x_rt, net.me, 1 - net.x)
        table(3, 0, z_rt, net.across_id, net.x)
        table(3, 1, x_rt, net.across_id, 1 - net.x)

    def chosen(self, which, near, far):
        rows = dot_f32(self.tabs[which, 0], flat(near), OUTER) + dot_f32(self.tabs[which, 1], flat(far), OUTER)
        return rows[: 2 * self.span].astype(jnp.bfloat16).reshape(2, self.span, -1)

    def share(self, unit, view):
        self.pending.setdefault(unit, []).extend([self.net.push(view, view, peer) for peer in self.net.mates])

    def route(self, unit):
        net, t = self.net, unit[0]
        kind, wide, thin = self.cols(unit)
        rows, send, other = self.rows[t], (self.send0, self.send1)[kind][t], (self.up, self.by)[kind][t]
        if t:
            self.side[unit].wait_recv()
        near, far = self.near[t][:, :, wide], other[:, :, thin]
        send[:, :, thin] = self.chosen(1 + 2 * kind, near, far)
        target = rows.at[net.core, net.x, :, :, wide] if kind == 0 else rows.at[net.core, :, net.y, :, wide]
        self.moved[unit] = net.push(send.at[:, :, thin], target, (net.beside, net.across)[kind])
        target[...] = self.chosen(2 * kind, near, far)
        self.share(unit, target)

    def last(self, unit):
        net, rows = self.net, self.rows[unit[0]]
        kind, wide, _ = self.cols(unit)
        self.moved[unit].wait_recv()
        if kind == 0:
            self.share(unit, rows.at[net.core, 1 - net.x, :, :, wide])
        else:
            self.share(unit, rows.at[net.core, :, 1 - net.y, :, wide])

    def settle(self, units):
        for unit in units:
            arrived(self.pending[unit])

    def first_half(self):
        u, rt = self.units, (0, 0)
        self.start()
        self.push_side(rt)
        self.push_side(u[0])
        self.tables()
        self.route(rt)
        self.push_side(u[1])
        self.route(u[0])
        self.push_side(u[2])
        self.route(u[1])
        self.push_side(u[3])
        self.last(rt)
        self.last(u[0])
        self.route(u[2])
        self.push_side(u[4])
        self.last(u[1])
        self.route(u[3])
        self.push_side(u[5])
        self.last(u[2])
        self.route(u[4])
        self.push_side(u[6])
        self.last(u[3])
        self.route(u[5])
        self.push_side(u[7])
        self.settle([rt] + u[:4])


def dispatch_kernel(depth, group, top, *refs):
    ins, rows, tabs = refs[:3], refs[3:6], refs[6]
    own_sem, send_sem, recv_sem = refs[21:]
    net = Net(depth, group, send_sem, recv_sem)
    step = Dispatch(net, top, ins, rows, tabs, refs[7:16], refs[16:21], own_sem)
    net.barrier()
    step.first_half()
    u = step.units
    for unit in u[6:]:
        step.route(unit)
    for unit in u[4:]:
        step.last(unit)
    step.settle(u[4:])
    net.finish()


def dispatch_scratch(depth, count, span, width):
    half, bf16 = width // 2, jnp.bfloat16
    dense = [pltpu.VMEM((depth, count, w), bf16) for w in (LANES, width, width) + (LANES, half, half) * 2]
    return dense + [pltpu.VMEM((2, span, w), bf16) for w in (LANES, half, half, half, half)]


def dispatch_copies(depth, group):
    return (2 * PARTS + 1) * (depth + 1 + 2 * (group - 1)) + 1


def semaphores(copies):
    return [pltpu.SemaphoreType.DMA((copies,)), pltpu.SemaphoreType.DMA((copies,))]


VMEM_SPEC = pl.BlockSpec(memory_space=pltpu.VMEM)
ANY_SPEC = pl.BlockSpec(memory_space=pl.ANY)


def dispatch(experts, group, top, capacity, routing, tokens, cotangent):
    depth = experts // 4
    count, width = tokens.shape
    span = depth * capacity
    bf16 = jnp.bfloat16
    return pl.pallas_call(
        functools.partial(dispatch_kernel, depth, group, top),
        out_shape=[
            jax.ShapeDtypeStruct((group, 2, 2, span, LANES), bf16),
            jax.ShapeDtypeStruct((group, 2, 2, span, width), bf16),
            jax.ShapeDtypeStruct((group, 2, 2, span, width), bf16),
            jax.ShapeDtypeStruct((4, 2, depth * count, LANES), bf16),
        ],
        in_specs=[VMEM_SPEC] * 3,
        out_specs=[VMEM_SPEC] * 4,
        scratch_shapes=dispatch_scratch(depth, count, span, width)
        + [pltpu.SemaphoreType.DMA((3,))]
        + semaphores(dispatch_copies(depth, group)),
        compiler_params=pltpu.CompilerParams(
            collective_id=0, has_side_effects=True, vmem_limit_bytes=VMEM_LIMIT
        ),
    )(routing, tokens, cotangent)


JOBS = ((0, 0),) + tuple((source, c) for source in (1, 2) for c in ORDER)


class Job:
    def __init__(self, net, depth, group, tabs, part, out, place, bufs):
        kind = int(2 * place >= PARTS)
        self.net, self.depth, self.group, self.tabs = net, depth, group, tabs
        self.part, self.out, self.kind = part, out, kind
        (self.mate, self.give, self.own, self.take, self.far, self.near, self.came, self.deep) = bufs
        width = self.give.shape[-1]
        self.cols, self.every = pl.ds(place * width, width), pl.ds(0, width)
        self.first, self.second = (net.beside, net.across) if kind == 0 else (net.across, net.beside)

    def pick(self, ref, lead, remote, cols):
        net = self.net
        if self.kind == 0:
            return ref.at[lead, 1 - net.x if remote else net.x, :, :, cols]
        return ref.at[lead, :, 1 - net.y if remote else net.y, :, cols]

    def exchange(self):
        net, group = self.net, self.group
        self.copies0 = []
        for remote in (True, False):
            self.copies0.append([
                net.push(
                    self.pick(self.part, (net.core + k) % group, remote, self.cols),
                    self.pick(self.mate, k - 1, remote, self.every),
                    net.mates[k - 1],
                )
                for k in range(1, group)
            ])

    def total(self, remote):
        acc = self.pick(self.part, self.net.core, remote, self.cols)[...].astype(jnp.float32)
        for k in range(1, self.group):
            acc = acc + self.pick(self.mate, k - 1, remote, self.every)[...].astype(jnp.float32)
        return acc.astype(jnp.bfloat16)

    def hop1(self):
        arrived(self.copies0[0])
        self.give[...] = self.total(True)
        self.copy1 = self.net.push(self.give, self.take, self.first)

    def keep(self):
        arrived(self.copies0[1])
        self.own[...] = self.total(False)

    def spread(self, part):
        rows, which = 2 * self.give.shape[1], 2 * self.kind
        mine = dot_f32(self.tabs[which, part, :, :rows], flat(self.own[...]))
        theirs = dot_f32(self.tabs[which + 1, part, :, :rows], flat(self.take[...]))
        return (mine + theirs).astype(jnp.bfloat16).reshape(self.far.shape)

    def hop2(self):
        self.copy1.wait_recv()
        self.far[...] = self.spread(1)
        self.copy2 = self.net.push(self.far, self.came, self.second)
        self.near[...] = self.spread(0)

    def hop3(self):
        net, depth = self.net, self.depth
        self.copy2.wait_recv()
        self.near[...] = (self.near[...].astype(jnp.float32) + self.came[...].astype(jnp.float32)).astype(jnp.bfloat16)
        self.copies3 = [
            net.push(self.near.at[(net.z + k) % depth], self.deep.at[net.z], net.deep[k - 1]) for k in range(1, depth)
        ]

    def sum(self):
        z, depth = self.net.z, self.depth
        arrived(self.copies3)
        acc = self.near[z].astype(jnp.float32)
        for k in range(1, depth):
            acc = acc + self.deep[(z + k) % depth].astype(jnp.float32)
        return acc

    def home(self):
        self.out[:, self.cols] = self.sum().astype(self.out.dtype)


def jobs_scratch(depth, group, count, span, width):
    bf16, chunk, bufs = jnp.bfloat16, width // PARTS, []
    for source, _ in JOBS:
        w = LANES if source == 0 else chunk
        bufs += [pltpu.VMEM((max(1, group - 1), 2, 2, span, w), bf16)]
        bufs += [pltpu.VMEM((2, span, w), bf16)] * 3
        bufs += [pltpu.VMEM((depth, count, w), bf16)] * 4
    return bufs


def jobs_copies(depth, group):
    return len(JOBS) * (2 * (group - 1) + 2 + depth - 1)


def make_jobs(net, depth, group, tabs, parts, outs, bufs):
    return [
        Job(net, depth, group, tabs, parts[source], outs[source], place, bufs[8 * i : 8 * i + 8])
        for i, (source, place) in enumerate(JOBS)
    ]


def combine_kernel(depth, group, *refs):
    tabs, parts, outs = refs[0], refs[1:4], refs[4:7]
    net = Net(depth, group, refs[-2], refs[-1])
    net.barrier()
    jobs = make_jobs(net, depth, group, tabs, parts, outs, refs[7:-2])
    for name in ("exchange", "hop1", "keep", "hop2", "hop3", "home"):
        for job in jobs:
            getattr(job, name)()
    net.finish()


def combine(experts, group, capacity, count, tabs, parts):
    depth = experts // 4
    width = parts[1].shape[-1]
    bf16 = jnp.bfloat16
    return pl.pallas_call(
        functools.partial(combine_kernel, depth, group),
        out_shape=[
            jax.ShapeDtypeStruct((count, LANES), jnp.float32),
            jax.ShapeDtypeStruct((count, width), bf16),
            jax.ShapeDtypeStruct((count, width), bf16),
        ],
        in_specs=[VMEM_SPEC] * 4,
        out_specs=[VMEM_SPEC] * 3,
        scratch_shapes=jobs_scratch(depth, group, count, depth * capacity, width)
        + semaphores(jobs_copies(depth, group)),
        compiler_params=pltpu.CompilerParams(
            collective_id=1, has_side_effects=True, vmem_limit_bytes=VMEM_LIMIT
        ),
    )(tabs, *parts)


def layer_kernel(depth, group, top, *refs):
    (routes, route_gates, tokens, cotangent, wg_hbm, wu_hbm, wd_hbm), refs = refs[:7], refs[1:]
    (mixed, token_grad, gate_grad, row_tok, row_back, hid_t, pre_t, upv_t) = refs[6:14]
    (wg, wu, wd, row_rt, row_cot, tabs, row_gate, gp, up, bh, hid, pre, upv, ext_part, out_part, back_part, acc, gate_cols) = refs[14:32]
    dense, routed = refs[32:41], refs[41:46]
    weight_sem, own_sem, send_sem, recv_sem = refs[-4:]
    rt, square = refs[-6:-4]
    bufs = refs[46:-6]
    ins = (rt, tokens, cotangent)
    net = Net(depth, group, send_sem, recv_sem)
    count = rt.shape[0]
    square[...] = jnp.zeros_like(square)
    square[:top, :count] = routes[...].astype(jnp.float32)
    square[top : 2 * top, :count] = route_gates[...].astype(jnp.float32)
    rt[...] = square[...].T[:count].astype(jnp.bfloat16)
    step = Dispatch(net, top, ins, (row_rt, row_tok, row_cot), tabs, dense, routed, own_sem)
    jobs = make_jobs(net, depth, group, tabs, (ext_part, out_part, back_part), (gate_cols, mixed, token_grad), bufs)
    ext, forward, back = jobs[0], jobs[1 : 1 + PARTS], jobs[1 + PARTS :]
    slots, ff, width = gp.shape[0], wg.shape[0], wg.shape[1]
    lead = row_tok.shape[:4]
    chunk = width // PARTS
    net.barrier()
    weights = []
    for i, (src, dst) in enumerate(((wg_hbm, wg), (wu_hbm, wu), (wd_hbm, wd))):
        copy = pltpu.make_async_copy(src.at[0], dst, weight_sem.at[i])
        weights.append(copy)

    for copy in weights:
        copy.start()
    step.first_half()
    units = step.units

    lane = lax.broadcasted_iota(jnp.int32, (slots, LANES), 1)
    routing = row_rt[...].reshape(slots, LANES).astype(jnp.float32)
    gates = pltpu.roll(routing, LANES - top, 1)
    named = (routing == net.me.astype(jnp.float32)) & (lane < top)
    row_gate[...] = jnp.broadcast_to(jnp.sum(jnp.where(named, gates, 0.0), axis=1, keepdims=True), (slots, LANES))

    for copy in weights:
        copy.wait()
    gp[...] = dot_f32(row_tok[...].reshape(slots, width), wg[...], INNER)
    step.last(units[4])
    step.route(units[6])
    up[...] = dot_f32(row_tok[...].reshape(slots, width), wu[...], INNER)
    step.route(units[7])
    step.last(units[5])

    rows = 16

    @pl.loop(0, slots // rows)
    def _(i):
        at = pl.ds(pl.multiple_of(i * rows, rows), rows)
        g = gp[at, :]
        hid[at, pl.ds(0, ff)] = (g * jax.nn.sigmoid(g) * up[at, :]).astype(jnp.bfloat16)

    step.last(units[6])
    step.last(units[7])
    step.settle(units[4:])
    acc[...] = jnp.zeros_like(acc)

    def out_cols(job):
        cols = job.cols
        value = dot_f32(hid[:, :ff], wd[:, cols])
        cot = row_cot[:, :, :, :, cols].reshape(slots, chunk).astype(jnp.float32)
        product = value * cot
        total = acc[...]
        for j in range(chunk // LANES):
            total = total + product[:, j * LANES : (j + 1) * LANES]
        acc[...] = total
        gate = row_gate[:, :1]
        out_part[:, :, :, :, cols] = (value * gate).astype(jnp.bfloat16).reshape(lead + (chunk,))
        row_back[:, :, :, :, cols] = (cot * gate).astype(jnp.bfloat16).reshape(lead + (chunk,))
        job.exchange()

    f = forward
    out_cols(f[0])
    out_cols(f[1])
    f[0].hop1()
    out_cols(f[2])
    f[1].hop1()
    out_cols(f[3])
    f[2].hop1()
    f[0].keep()
    f[1].keep()

    row_grad = jnp.sum(acc[...], axis=1, keepdims=True)
    row_high = row_grad.astype(jnp.bfloat16).astype(jnp.float32)
    row_low = row_grad - row_high
    columns = jnp.where(lane == net.me, row_high, jnp.where(lane == LANES // 2 + net.me, row_low, 0.0))
    ext_part[...] = columns.astype(jnp.bfloat16).reshape(ext_part.shape)
    ext.exchange()
    bh[...] = dot_f32(row_back[...].reshape(slots, width), wd[...], INNER)
    f[3].hop1()
    ext.hop1()
    f[2].keep()
    f[3].keep()
    ext.keep()
    f[0].hop2()
    f[1].hop2()

    @pl.loop(0, slots // rows)
    def _(i):
        at = pl.ds(pl.multiple_of(i * rows, rows), rows)
        g, b = gp[at, :], bh[at, :]
        s = jax.nn.sigmoid(g)
        pre[at, pl.ds(0, ff)] = (b * up[at, :] * s * (1.0 + g * (1.0 - s))).astype(jnp.bfloat16)
        upv[at, pl.ds(0, ff)] = (b * g * s).astype(jnp.bfloat16)

    f[2].hop2()
    f[3].hop2()
    ext.hop2()

    def back_cols(job):
        cols = job.cols
        value = dot_f32(pre[:, :ff], wg[:, cols]) + dot_f32(upv[:, :ff], wu[:, cols])
        back_part[:, :, :, :, cols] = value.astype(jnp.bfloat16).reshape(lead + (chunk,))
        job.exchange()

    b = back
    back_cols(b[0])
    f[0].hop3()
    back_cols(b[1])
    b[0].hop1()
    f[1].hop3()
    b[0].keep()
    back_cols(b[2])
    b[1].hop1()
    f[2].hop3()
    b[1].keep()
    back_cols(b[3])
    b[2].hop1()
    f[3].hop3()
    ext.hop3()
    b[2].keep()
    b[0].hop2()
    b[3].hop1()
    b[3].keep()
    b[1].hop2()
    b[2].hop2()
    b[0].hop3()
    b[3].hop2()
    b[1].hop3()
    b[2].hop3()
    b[3].hop3()
    for src, dst in ((hid, hid_t), (pre, pre_t), (upv, upv_t)):
        dst[...] = src[...].T[:ff]
    for job in [ext] + forward:
        job.home()
    lane = lax.broadcasted_iota(jnp.int32, (count, LANES), 1)
    cols = gate_cols[...] + pltpu.roll(gate_cols[...], LANES // 2, 1)
    routing = rt[...].astype(jnp.float32)
    grads = jnp.zeros((count, LANES), jnp.float32)
    for k in range(top):
        hit = (routing[:, k : k + 1] == lane.astype(jnp.float32)) & (lane < LANES // 2)
        grads = jnp.where(lane == k, jnp.sum(jnp.where(hit, cols, 0.0), axis=1, keepdims=True), grads)
    square[:count, :] = grads
    gate_grad[...] = square[...].T[: gate_grad.shape[0]]
    for job in back:
        job.home()
    net.finish()


def layer(experts, group, top, capacity, routes, route_gates, tokens, cotangent, w_gate, w_up, w_down):
    depth = experts // 4
    count, width = tokens.shape
    ff = w_gate.shape[1]
    span = depth * capacity
    slots = group * 4 * span
    wide = -(-ff // LANES) * LANES
    bf16, f32 = jnp.bfloat16, jnp.float32
    blocks = (group, 2, 2, span)
    scratch = [
        pltpu.VMEM((ff, width), bf16), pltpu.VMEM((ff, width), bf16), pltpu.VMEM((ff, width), bf16),
        pltpu.VMEM(blocks + (LANES,), bf16), pltpu.VMEM(blocks + (width,), bf16),
        pltpu.VMEM((4, 2, depth * count, LANES), bf16), pltpu.VMEM((slots, LANES), f32),
        pltpu.VMEM((slots, ff), f32), pltpu.VMEM((slots, ff), f32), pltpu.VMEM((slots, ff), f32),
        pltpu.VMEM((slots, wide), bf16), pltpu.VMEM((slots, wide), bf16), pltpu.VMEM((slots, wide), bf16),
        pltpu.VMEM(blocks + (LANES,), bf16), pltpu.VMEM(blocks + (width,), bf16), pltpu.VMEM(blocks + (width,), bf16),
        pltpu.VMEM((slots, LANES), f32), pltpu.VMEM((count, LANES), f32),
    ]
    copies = dispatch_copies(depth, group) + jobs_copies(depth, group)
    return pl.pallas_call(
        functools.partial(layer_kernel, depth, group, top),
        out_shape=[
            jax.ShapeDtypeStruct((count, width), bf16),
            jax.ShapeDtypeStruct((count, width), bf16),
            jax.ShapeDtypeStruct((8, LANES), f32),
            jax.ShapeDtypeStruct(blocks + (width,), bf16),
            jax.ShapeDtypeStruct(blocks + (width,), bf16),
        ] + [jax.ShapeDtypeStruct((ff, slots), bf16)] * 3,
        in_specs=[VMEM_SPEC] * 2 + [ANY_SPEC] * 5,
        out_specs=[VMEM_SPEC] * 8,
        scratch_shapes=scratch
        + dispatch_scratch(depth, count, span, width)
        + jobs_scratch(depth, group, count, span, width)
        + [pltpu.VMEM((count, LANES), bf16), pltpu.VMEM((LANES, LANES), f32)]
        + [pltpu.SemaphoreType.DMA((3,)), pltpu.SemaphoreType.DMA((3,))]
        + semaphores(copies),
        compiler_params=pltpu.CompilerParams(
            collective_id=2, has_side_effects=True, vmem_limit_bytes=VMEM_LIMIT
        ),
    )(routes.T, route_gates.T, tokens, cotangent, w_gate, w_up, w_down)


def weight_kernel(hid_t, pre_t, upv_t, rows_in, rows_back, mixed_in, token_in, route_in, down, gate, up, mixed, token_grad, route_grad):
    down[0] = dot_f32(hid_t[...], rows_back[...])
    gate[0] = dot_f32(pre_t[...], rows_in[...])
    up[0] = dot_f32(upv_t[...], rows_in[...])
    mixed[...] = mixed_in[...]
    token_grad[...] = token_in[...]
    route_grad[...] = route_in[: route_grad.shape[0], : route_grad.shape[1]]


def weight_grads(top, hid_t, pre_t, upv_t, rows_in, rows_back, mixed, token_grad, route_grad):
    ff, slots = hid_t.shape
    count, width = mixed.shape
    chunk = 256
    whole = lambda array: pl.BlockSpec(array.shape, lambda i: (0, 0))
    columns = lambda array: pl.BlockSpec((array.shape[0], chunk), lambda i: (0, i))
    wide = pl.BlockSpec((1, ff, chunk), lambda i: (0, 0, i))
    grads = jax.ShapeDtypeStruct((1, ff, width), jnp.float32)
    route = jax.ShapeDtypeStruct((top, count), jnp.float32)
    return pl.pallas_call(
        weight_kernel,
        grid=(width // chunk,),
        out_shape=[grads, grads, grads, mixed, token_grad, route],
        in_specs=[whole(hid_t)] * 3 + [columns(rows_in)] * 2 + [columns(mixed)] * 2 + [whole(route_grad)],
        out_specs=[wide] * 3 + [columns(mixed)] * 2 + [whole(route)],
        cost_estimate=pl.CostEstimate(
            flops=6 * slots * ff * width, bytes_accessed=12 * ff * width, transcendentals=0
        ),
        compiler_params=pltpu.CompilerParams(vmem_limit_bytes=VMEM_LIMIT),
    )(hid_t, pre_t, upv_t, rows_in, rows_back, mixed, token_grad, route_grad)


def per_device(tokens, cotangent, route_gates, routes, w_gate, w_up, w_down):
    experts, group = lax.axis_size("expert"), lax.axis_size("dp")
    token_count, top_count = routes.shape
    width = tokens.shape[1]
    capacity = max(2, token_count * top_count * 4 // (3 * experts))
    slots = experts * group * capacity
    gate_shard, up_shard, down_shard = (w_gate[0], w_up[0], w_down[0])
    me = lax.axis_index("expert")

    if 2 * slots * width * tokens.dtype.itemsize <= FUSED_LIMIT:
        mixed, token_grad, gate_grad, rows_in, rows_back, hid_t, pre_t, upv_t = layer(
            experts, group, top_count, capacity, routes, route_gates, tokens, cotangent, w_gate, w_up, w_down
        )
        rows_in, rows_back = rows_in.reshape(slots, width), rows_back.reshape(slots, width)
        grad_down, grad_gate, grad_up, mixed, token_grad, gate_grad = weight_grads(
            top_count, hid_t, pre_t, upv_t, rows_in, rows_back, mixed, token_grad, gate_grad
        )
        return (mixed, token_grad, gate_grad.T, grad_gate, grad_up, grad_down)
    routing = jnp.concatenate([routes.astype(jnp.bfloat16), route_gates], axis=1)
    routing = jnp.pad(routing, ((0, 0), (0, LANES - 2 * top_count)))
    row_rt, row_tok, row_cot, tabs = dispatch(experts, group, top_count, capacity, routing, tokens, cotangent)
    shape = row_tok.shape
    row_rt = row_rt.reshape(slots, LANES).astype(jnp.float32)
    rows_in, rows_cot = row_tok.reshape(slots, width), row_cot.reshape(slots, width)
    named = row_rt[:, :top_count] == me.astype(jnp.float32)
    row_gate = jnp.sum(jnp.where(named, row_rt[:, top_count : 2 * top_count], 0.0), axis=1)[:, None]

    gate_pre = dot_f32(rows_in, gate_shard, INNER)
    up_pre = dot_f32(rows_in, up_shard, INNER)
    sig = jax.nn.sigmoid(gate_pre)
    hidden = (gate_pre * sig * up_pre).astype(jnp.bfloat16)
    out_rows = dot_f32(hidden, down_shard)
    row_grad = jnp.sum(out_rows * rows_cot.astype(jnp.float32), axis=1)[:, None]
    out_part = (out_rows * row_gate).astype(jnp.bfloat16)
    lane = jnp.arange(LANES, dtype=jnp.int32)[None, :]
    row_high = row_grad.astype(jnp.bfloat16)
    row_low = (row_grad - row_high.astype(jnp.float32)).astype(jnp.bfloat16)
    zero = jnp.zeros((), jnp.bfloat16)
    grad_cols = jnp.where(lane == me, row_high, jnp.where(lane == LANES // 2 + me, row_low, zero))
    rows_back = (rows_cot.astype(jnp.float32) * row_gate).astype(jnp.bfloat16)
    back_hidden = dot_f32(rows_back, down_shard, INNER)
    grad_pre = (back_hidden * up_pre * sig * (1.0 + gate_pre * (1.0 - sig))).astype(jnp.bfloat16)
    grad_upv = (back_hidden * gate_pre * sig).astype(jnp.bfloat16)
    back_part = (dot_f32(grad_pre, gate_shard) + dot_f32(grad_upv, up_shard)).astype(jnp.bfloat16)
    gate_cols, mixed, token_grad = combine(
        experts, group, capacity, token_count, tabs,
        [grad_cols.reshape(shape[:4] + (LANES,)), out_part.reshape(shape), back_part.reshape(shape)],
    )
    grad_down = dot_f32(hidden, rows_back, OUTER)
    grad_gate = dot_f32(grad_pre, rows_in, OUTER)
    grad_up = dot_f32(grad_upv, rows_in, OUTER)
    column = lane[:, None, :] % (LANES // 2)
    gate_grad = jnp.sum(jnp.where(routes[:, :, None] == column, gate_cols[:, None, :], 0.0), axis=2)
    return (mixed, token_grad, gate_grad, grad_gate[None], grad_up[None], grad_down[None])


def solution(mesh):
    row = P(("expert", "dp"), None)
    wide = P("expert", "dp", None)
    return jax.shard_map(
        per_device,
        mesh=mesh,
        in_specs=(row, row, row, row, wide, wide, wide),
        out_specs=(row, row, row, wide, wide, wide),
        check_vma=False,
    )
```

```python
import functools

import jax
import jax.numpy as jnp
from jax import lax
from jax.experimental import pallas as pl
from jax.experimental.pallas import tpu as pltpu
from jax.sharding import PartitionSpec as P

INNER = (((1,), (1,)), ((), ()))
OUTER = (((0,), (0,)), ((), ()))
LANES = 128
VMEM_LIMIT = 60 * 1024 * 1024
FUSED_LIMIT = 4 * 1024 * 1024
PARTS = 4
ORDER = (0, 2, 1, 3)


def dot_f32(left, right, dims=(((1,), (0,)), ((), ()))):
    return lax.dot_general(left, right, dims, preferred_element_type=jnp.float32)


class Net:
    def __init__(self, depth, group, send_sem, recv_sem):
        me, core = lax.axis_index("expert"), lax.axis_index("dp")
        z, y, x = me // 4, (me // 2) % 2, me % 2
        self.me, self.core, self.z, self.y, self.x = me, core, z, y, x

        def at(zz, yy, xx, cc):
            return (zz * 4 + yy * 2 + xx, cc)

        self.deep = [at((z + k) % depth, y, x, core) for k in range(1, depth)]
        self.across, self.beside = at(z, 1 - y, x, core), at(z, y, 1 - x, core)
        self.mates = [at(z, y, x, (core + k) % group) for k in range(1, group)]
        self.across_id, self.beside_id = self.across[0], self.beside[0]
        self.send_sem, self.recv_sem = send_sem, recv_sem
        self.sent, self.used = [], 0
        self.depth, self.chain = depth, []
        self.above, self.below = at((z + 1) % depth, y, x, core), at((z + depth - 1) % depth, y, x, core)

    def barrier(self):
        peers = self.deep + [self.across, self.beside] + self.mates
        barrier = pltpu.get_barrier_semaphore()
        for peer in peers:
            pl.semaphore_signal(barrier, inc=1, device_id=peer, device_id_type=pl.DeviceIdType.MESH)
        pl.semaphore_wait(barrier, len(peers))

    def push(self, src, dst, peer):
        index = self.used
        self.used += 1
        copy = pltpu.make_async_remote_copy(
            src_ref=src, dst_ref=dst, send_sem=self.send_sem.at[index], recv_sem=self.recv_sem.at[index],
            device_id=peer, device_id_type=pl.DeviceIdType.MESH,
        )
        copy.start()
        self.sent.append(copy)
        return copy

    def link(self, src, dst, peer, going, coming):
        index = self.used
        self.used += 1
        copy = pltpu.make_async_remote_copy(
            src_ref=src, dst_ref=dst, send_sem=self.send_sem.at[index], recv_sem=self.recv_sem.at[index],
            device_id=peer, device_id_type=pl.DeviceIdType.MESH,
        )
        pl.when(going)(copy.start)
        self.chain.append((going, copy))
        return lambda: pl.when(coming)(copy.wait_recv)

    def finish(self):
        for going, copy in self.chain:
            pl.when(going)(copy.wait_send)
        for copy in self.sent:
            copy.wait_send()


def arrived(copies):
    for copy in copies:
        copy.wait_recv()


def flat(value):
    return value.reshape(-1, value.shape[-1])


class Dispatch:
    def __init__(self, net, top, ins, rows, tabs, dense, routed, own_sem):
        self.net, self.top, self.ins, self.rows, self.tabs = net, top, ins, rows, tabs
        self.near, self.up, self.by = dense[:3], dense[3:6], dense[6:9]
        self.send0, self.send1 = (routed[0], routed[1], routed[2]), (None, routed[3], routed[4])
        self.own_sem = own_sem
        self.half, self.chunk = ins[1].shape[1] // 2, ins[1].shape[1] // PARTS
        self.span = rows[0].shape[3]
        self.units = [(t, c) for t in (1, 2) for c in ORDER]
        self.pending, self.moved, self.deep, self.side = {}, {}, {}, {}

    def cols(self, unit):
        t, c = unit
        if t == 0:
            return 0, pl.ds(0, LANES), pl.ds(0, LANES)
        kind = int(2 * c >= PARTS)
        return kind, pl.ds(c * self.chunk, self.chunk), pl.ds(c * self.chunk - kind * self.half, self.chunk)

    def start(self):
        net = self.net
        own = []
        for t in range(3):
            copy = pltpu.make_async_copy(self.ins[t], self.near[t].at[net.z], self.own_sem.at[t])
            copy.start()
            own.append(copy)
        for copy in own:
            copy.wait()

    def forward(self, unit, stage):
        net, z, depth = self.net, self.net.z, self.net.depth
        near, wide = self.near[unit[0]], self.cols(unit)[1]
        if stage > 1:
            for wait in self.deep[unit]:
                wait()
        up, down = z - stage + 1, z + stage - 1
        low, high = jnp.maximum(up, 0), jnp.minimum(down, depth - 1)
        rising, falling = near.at[low, :, wide], near.at[high, :, wide]
        self.deep[unit] = [
            net.link(rising, rising, net.above, (up >= 0) & (z + 1 < depth), z - stage >= 0),
            net.link(falling, falling, net.below, (down < depth) & (z >= 1), z + stage < depth),
        ]

    def push_side(self, unit):
        net, t = self.net, unit[0]
        kind, wide, thin = self.cols(unit)
        for wait in self.deep[unit]:
            wait()
        if t == 0:
            self.side[unit] = net.push(self.near[t], self.up[t], net.across)
            self.side_by = net.push(self.near[t], self.by[t], net.beside)
        elif kind == 0:
            self.side[unit] = net.push(self.near[t].at[:, :, wide], self.up[t].at[:, :, thin], net.across)
        else:
            self.side[unit] = net.push(self.near[t].at[:, :, wide], self.by[t].at[:, :, thin], net.beside)

    def tables(self):
        net, span, count = self.net, self.span, self.ins[0].shape[0]
        self.side[0, 0].wait_recv()
        self.side_by.wait_recv()
        depth = self.near[0].shape[0]
        total = depth * count
        lane = lax.broadcasted_iota(jnp.int32, (total, LANES), 1)
        row = lax.broadcasted_iota(jnp.int32, (total, LANES), 0)
        down, right = lax.broadcasted_iota(jnp.int32, (total, total), 0), lax.broadcasted_iota(jnp.int32, (total, total), 1)
        kcap = jnp.zeros((total, LANES), jnp.int32)
        first = jnp.zeros((total, total), jnp.int32)
        for k in range(1, depth):
            kcap = jnp.where(row >= k * count, k * (span // depth), kcap)
            first = jnp.where(down >= k * count, k * count, first)
        tri = ((right < down) & (right >= first)).astype(jnp.float32).astype(jnp.bfloat16)

        def table(which, part, source, expert, base):
            routing = flat(source[...]).astype(jnp.float32)
            named = (routing == expert.astype(jnp.float32)) & (lane < self.top)
            used = jnp.sum(named.astype(jnp.float32), axis=1, keepdims=True)
            used = jnp.broadcast_to(used, lane.shape)
            rank = dot_f32(tri, used.astype(jnp.bfloat16))
            slot = rank + (kcap + base * span).astype(jnp.float32)
            hit = (used > 0.5) & (slot == lane.astype(jnp.float32))
            self.tabs[which, part] = hit.astype(jnp.float32).astype(jnp.bfloat16)

        z_rt, y_rt, x_rt = self.near[0], self.up[0], self.by[0]
        table(0, 0, z_rt, net.me, net.y)
        table(0, 1, y_rt, net.me, 1 - net.y)
        table(1, 0, z_rt, net.beside_id, net.y)
        table(1, 1, y_rt, net.beside_id, 1 - net.y)
        table(2, 0, z_rt, net.me, net.x)
        table(2, 1, x_rt, net.me, 1 - net.x)
        table(3, 0, z_rt, net.across_id, net.x)
        table(3, 1, x_rt, net.across_id, 1 - net.x)

    def chosen(self, which, near, far):
        rows = dot_f32(self.tabs[which, 0], flat(near), OUTER) + dot_f32(self.tabs[which, 1], flat(far), OUTER)
        return rows[: 2 * self.span].astype(jnp.bfloat16).reshape(2, self.span, -1)

    def share(self, unit, view):
        self.pending.setdefault(unit, []).extend([self.net.push(view, view, peer) for peer in self.net.mates])

    def route(self, unit):
        net, t = self.net, unit[0]
        kind, wide, thin = self.cols(unit)
        rows, send, other = self.rows[t], (self.send0, self.send1)[kind][t], (self.up, self.by)[kind][t]
        if t:
            self.side[unit].wait_recv()
        near, far = self.near[t][:, :, wide], other[:, :, thin]
        send[:, :, thin] = self.chosen(1 + 2 * kind, near, far)
        target = rows.at[net.core, net.x, :, :, wide] if kind == 0 else rows.at[net.core, :, net.y, :, wide]
        self.moved[unit] = net.push(send.at[:, :, thin], target, (net.beside, net.across)[kind])
        target[...] = self.chosen(2 * kind, near, far)
        self.share(unit, target)

    def last(self, unit):
        net, rows = self.net, self.rows[unit[0]]
        kind, wide, _ = self.cols(unit)
        self.moved[unit].wait_recv()
        if kind == 0:
            self.share(unit, rows.at[net.core, 1 - net.x, :, :, wide])
        else:
            self.share(unit, rows.at[net.core, :, 1 - net.y, :, wide])

    def settle(self, units):
        for unit in units:
            arrived(self.pending[unit])

    def first_half(self):
        u, rt = self.units, (0, 0)
        early, late, depth = [rt] + u[:4], u[4:], self.net.depth
        self.start()
        for unit in early:
            self.forward(unit, 1)
        for stage in range(2, depth + 1):
            for unit in early if stage < depth else []:
                self.forward(unit, stage)
            for unit in late if stage < depth else []:
                self.forward(unit, stage - 1)
        self.push_side(rt)
        self.push_side(u[0])
        self.push_side(u[1])
        for unit in late[:2]:
            self.forward(unit, depth - 1)
        self.tables()
        self.route(rt)
        self.push_side(u[2])
        self.push_side(u[3])
        for unit in late[2:]:
            self.forward(unit, depth - 1)
        self.route(u[0])
        self.route(u[1])
        self.route(u[2])
        self.push_side(u[4])
        self.route(u[3])
        self.last(rt)
        self.push_side(u[5])
        self.last(u[0])
        self.last(u[1])
        self.push_side(u[6])
        self.push_side(u[7])
        self.last(u[2])
        self.route(u[4])
        self.last(u[3])
        self.route(u[5])
        self.settle([rt] + u[:4])


def dispatch_kernel(depth, group, top, *refs):
    ins, rows, tabs = refs[:3], refs[3:6], refs[6]
    own_sem, send_sem, recv_sem = refs[21:]
    net = Net(depth, group, send_sem, recv_sem)
    step = Dispatch(net, top, ins, rows, tabs, refs[7:16], refs[16:21], own_sem)
    net.barrier()
    step.first_half()
    u = step.units
    for unit in u[6:]:
        step.route(unit)
    for unit in u[4:]:
        step.last(unit)
    step.settle(u[4:])
    net.finish()


def dispatch_scratch(depth, count, span, width):
    half, bf16 = width // 2, jnp.bfloat16
    dense = [pltpu.VMEM((depth, count, w), bf16) for w in (LANES, width, width) + (LANES, half, half) * 2]
    return dense + [pltpu.VMEM((2, span, w), bf16) for w in (LANES, half, half, half, half)]


def dispatch_copies(depth, group):
    return (2 * PARTS + 1) * (2 * depth + 2 * (group - 1)) + 1


def semaphores(copies):
    return [pltpu.SemaphoreType.DMA((copies,)), pltpu.SemaphoreType.DMA((copies,))]


VMEM_SPEC = pl.BlockSpec(memory_space=pltpu.VMEM)
ANY_SPEC = pl.BlockSpec(memory_space=pl.ANY)


def dispatch(experts, group, top, capacity, routing, tokens, cotangent):
    depth = experts // 4
    count, width = tokens.shape
    span = depth * capacity
    bf16 = jnp.bfloat16
    return pl.pallas_call(
        functools.partial(dispatch_kernel, depth, group, top),
        out_shape=[
            jax.ShapeDtypeStruct((group, 2, 2, span, LANES), bf16),
            jax.ShapeDtypeStruct((group, 2, 2, span, width), bf16),
            jax.ShapeDtypeStruct((group, 2, 2, span, width), bf16),
            jax.ShapeDtypeStruct((4, 2, depth * count, LANES), bf16),
        ],
        in_specs=[VMEM_SPEC] * 3,
        out_specs=[VMEM_SPEC] * 4,
        scratch_shapes=dispatch_scratch(depth, count, span, width)
        + [pltpu.SemaphoreType.DMA((3,))]
        + semaphores(dispatch_copies(depth, group)),
        compiler_params=pltpu.CompilerParams(
            collective_id=0, has_side_effects=True, vmem_limit_bytes=VMEM_LIMIT
        ),
    )(routing, tokens, cotangent)


JOBS = ((0, 0),) + tuple((source, c) for source in (1, 2) for c in ORDER)


class Job:
    def __init__(self, net, depth, group, tabs, part, out, place, bufs):
        kind = int(2 * place >= PARTS)
        self.net, self.depth, self.group, self.tabs = net, depth, group, tabs
        self.part, self.out, self.kind = part, out, kind
        (self.mate, self.give, self.own, self.take, self.far, self.near, self.came, self.deep) = bufs
        width = self.give.shape[-1]
        self.cols, self.every = pl.ds(place * width, width), pl.ds(0, width)
        self.first, self.second = (net.beside, net.across) if kind == 0 else (net.across, net.beside)

    def pick(self, ref, lead, remote, cols):
        net = self.net
        if self.kind == 0:
            return ref.at[lead, 1 - net.x if remote else net.x, :, :, cols]
        return ref.at[lead, :, 1 - net.y if remote else net.y, :, cols]

    def exchange(self):
        net, group = self.net, self.group
        self.copies0 = []
        for remote in (True, False):
            self.copies0.append([
                net.push(
                    self.pick(self.part, (net.core + k) % group, remote, self.cols),
                    self.pick(self.mate, k - 1, remote, self.every),
                    net.mates[k - 1],
                )
                for k in range(1, group)
            ])

    def total(self, remote):
        acc = self.pick(self.part, self.net.core, remote, self.cols)[...].astype(jnp.float32)
        for k in range(1, self.group):
            acc = acc + self.pick(self.mate, k - 1, remote, self.every)[...].astype(jnp.float32)
        return acc.astype(jnp.bfloat16)

    def hop1(self):
        arrived(self.copies0[0])
        self.give[...] = self.total(True)
        self.copy1 = self.net.push(self.give, self.take, self.first)

    def keep(self):
        arrived(self.copies0[1])
        self.own[...] = self.total(False)

    def spread(self, part):
        rows, which = 2 * self.give.shape[1], 2 * self.kind
        mine = dot_f32(self.tabs[which, part, :, :rows], flat(self.own[...]))
        theirs = dot_f32(self.tabs[which + 1, part, :, :rows], flat(self.take[...]))
        return (mine + theirs).astype(jnp.bfloat16).reshape(self.far.shape)

    def hop2(self):
        self.copy1.wait_recv()
        self.far[...] = self.spread(1)
        self.copy2 = self.net.push(self.far, self.came, self.second)
        self.near[...] = self.spread(0)

    def hop3(self):
        self.copy2.wait_recv()
        self.near[...] = (self.near[...].astype(jnp.float32) + self.came[...].astype(jnp.float32)).astype(jnp.bfloat16)
        self.up_wait, self.down_wait = {}, {}

    def add(self, block, side):
        self.near[block] = (self.near[block].astype(jnp.float32) + self.deep[side, block].astype(jnp.float32)).astype(jnp.bfloat16)

    def along(self, stage):
        net, z, depth = self.net, self.net.z, self.depth
        up, down = depth - 1 - stage, stage
        for block, side, peer, passing, going, coming in (
            (up, 0, net.above, (z > 0) & (z < up), z < up, (z > 0) & (z <= up)),
            (down, 1, net.below, (z < depth - 1) & (z > down), z > down, (z < depth - 1) & (z >= down)),
        ):
            copy = pltpu.make_async_remote_copy(
                src_ref=self.near.at[block], dst_ref=self.deep.at[side, block],
                send_sem=net.send_sem.at[net.used], recv_sem=net.recv_sem.at[net.used],
                device_id=peer, device_id_type=pl.DeviceIdType.MESH,
            )
            net.used += 1

            @pl.when(passing)
            def _():
                copy.wait_recv()
                self.add(block, side)

            pl.when(going)(copy.start)
            net.chain.append((going, copy))
            (self.up_wait, self.down_wait)[side][block] = copy

    def sum(self):
        z, depth = self.net.z, self.depth
        for side, waits in ((0, self.up_wait), (1, self.down_wait)):
            for block, copy in waits.items():

                @pl.when(z == block)
                def _():
                    copy.wait_recv()
                    self.add(block, side)

        return self.near[z].astype(jnp.float32)

    def home(self):
        self.out[:, self.cols] = self.sum().astype(self.out.dtype)


def jobs_scratch(depth, group, count, span, width):
    bf16, chunk, bufs = jnp.bfloat16, width // PARTS, []
    for source, _ in JOBS:
        w = LANES if source == 0 else chunk
        bufs += [pltpu.VMEM((max(1, group - 1), 2, 2, span, w), bf16)]
        bufs += [pltpu.VMEM((2, span, w), bf16)] * 3
        bufs += [pltpu.VMEM((depth, count, w), bf16)] * 3
        bufs += [pltpu.VMEM((2, depth, count, w), bf16)]
    return bufs


def jobs_copies(depth, group):
    return len(JOBS) * (2 * (group - 1) + 2 * depth)


def make_jobs(net, depth, group, tabs, parts, outs, bufs):
    return [
        Job(net, depth, group, tabs, parts[source], outs[source], place, bufs[8 * i : 8 * i + 8])
        for i, (source, place) in enumerate(JOBS)
    ]


def combine_kernel(depth, group, *refs):
    tabs, parts, outs = refs[0], refs[1:4], refs[4:7]
    net = Net(depth, group, refs[-2], refs[-1])
    net.barrier()
    jobs = make_jobs(net, depth, group, tabs, parts, outs, refs[7:-2])
    for name in ("exchange", "hop1", "keep", "hop2", "hop3"):
        for job in jobs:
            getattr(job, name)()
    for stage in range(depth - 1):
        for job in jobs:
            job.along(stage)
    for job in jobs:
        job.home()
    net.finish()


def combine(experts, group, capacity, count, tabs, parts):
    depth = experts // 4
    width = parts[1].shape[-1]
    bf16 = jnp.bfloat16
    return pl.pallas_call(
        functools.partial(combine_kernel, depth, group),
        out_shape=[
            jax.ShapeDtypeStruct((count, LANES), jnp.float32),
            jax.ShapeDtypeStruct((count, width), bf16),
            jax.ShapeDtypeStruct((count, width), bf16),
        ],
        in_specs=[VMEM_SPEC] * 4,
        out_specs=[VMEM_SPEC] * 3,
        scratch_shapes=jobs_scratch(depth, group, count, depth * capacity, width)
        + semaphores(jobs_copies(depth, group)),
        compiler_params=pltpu.CompilerParams(
            collective_id=1, has_side_effects=True, vmem_limit_bytes=VMEM_LIMIT
        ),
    )(tabs, *parts)


def layer_kernel(depth, group, top, *refs):
    (routes, route_gates, tokens, cotangent, wg_hbm, wu_hbm, wd_hbm), refs = refs[:7], refs[1:]
    (mixed, token_grad, gate_grad, row_tok, row_back, hid_t, pre_t, upv_t) = refs[6:14]
    (wg, wu, wd, row_rt, row_cot, tabs, row_gate, gp, up, bh, hid, pre, upv, ext_part, out_part, back_part, acc, gate_cols) = refs[14:32]
    dense, routed = refs[32:41], refs[41:46]
    weight_sem, own_sem, send_sem, recv_sem = refs[-4:]
    rt, square = refs[-6:-4]
    bufs = refs[46:-6]
    ins = (rt, tokens, cotangent)
    net = Net(depth, group, send_sem, recv_sem)
    count = rt.shape[0]
    square[...] = jnp.zeros_like(square)
    square[:top, :count] = routes[...].astype(jnp.float32)
    square[top : 2 * top, :count] = route_gates[...].astype(jnp.float32)
    rt[...] = square[...].T[:count].astype(jnp.bfloat16)
    step = Dispatch(net, top, ins, (row_rt, row_tok, row_cot), tabs, dense, routed, own_sem)
    jobs = make_jobs(net, depth, group, tabs, (ext_part, out_part, back_part), (gate_cols, mixed, token_grad), bufs)
    ext, forward, back = jobs[0], jobs[1 : 1 + PARTS], jobs[1 + PARTS :]
    slots, ff, width = gp.shape[0], wg.shape[0], wg.shape[1]
    lead = row_tok.shape[:4]
    chunk = width // PARTS
    net.barrier()
    weights = []
    for i, (src, dst) in enumerate(((wg_hbm, wg), (wu_hbm, wu), (wd_hbm, wd))):
        copy = pltpu.make_async_copy(src.at[0], dst, weight_sem.at[i])
        weights.append(copy)

    for copy in weights:
        copy.start()
    step.first_half()
    units = step.units

    lane = lax.broadcasted_iota(jnp.int32, (slots, LANES), 1)
    routing = row_rt[...].reshape(slots, LANES).astype(jnp.float32)
    gates = pltpu.roll(routing, LANES - top, 1)
    named = (routing == net.me.astype(jnp.float32)) & (lane < top)
    row_gate[...] = jnp.broadcast_to(jnp.sum(jnp.where(named, gates, 0.0), axis=1, keepdims=True), (slots, LANES))

    for copy in weights:
        copy.wait()
    gp[...] = dot_f32(row_tok[...].reshape(slots, width), wg[...], INNER)
    step.last(units[4])
    step.route(units[6])
    up[...] = dot_f32(row_tok[...].reshape(slots, width), wu[...], INNER)
    step.route(units[7])
    step.last(units[5])

    rows = 16

    @pl.loop(0, slots // rows)
    def _(i):
        at = pl.ds(pl.multiple_of(i * rows, rows), rows)
        g = gp[at, :]
        hid[at, pl.ds(0, ff)] = (g * jax.nn.sigmoid(g) * up[at, :]).astype(jnp.bfloat16)

    step.last(units[6])
    step.last(units[7])
    step.settle(units[4:])
    acc[...] = jnp.zeros_like(acc)

    def out_cols(job):
        cols = job.cols
        value = dot_f32(hid[:, :ff], wd[:, cols])
        cot = row_cot[:, :, :, :, cols].reshape(slots, chunk).astype(jnp.float32)
        product = value * cot
        total = acc[...]
        for j in range(chunk // LANES):
            total = total + product[:, j * LANES : (j + 1) * LANES]
        acc[...] = total
        gate = row_gate[:, :1]
        out_part[:, :, :, :, cols] = (value * gate).astype(jnp.bfloat16).reshape(lead + (chunk,))
        row_back[:, :, :, :, cols] = (cot * gate).astype(jnp.bfloat16).reshape(lead + (chunk,))
        job.exchange()

    f = forward
    out_cols(f[0])
    out_cols(f[1])
    f[0].hop1()
    out_cols(f[2])
    f[1].hop1()
    out_cols(f[3])
    f[2].hop1()
    f[0].keep()
    f[1].keep()

    row_grad = jnp.sum(acc[...], axis=1, keepdims=True)
    row_high = row_grad.astype(jnp.bfloat16).astype(jnp.float32)
    row_low = row_grad - row_high
    columns = jnp.where(lane == net.me, row_high, jnp.where(lane == LANES // 2 + net.me, row_low, 0.0))
    ext_part[...] = columns.astype(jnp.bfloat16).reshape(ext_part.shape)
    ext.exchange()
    bh[...] = dot_f32(row_back[...].reshape(slots, width), wd[...], INNER)
    f[3].hop1()
    ext.hop1()
    f[2].keep()
    f[3].keep()
    ext.keep()
    f[0].hop2()
    f[1].hop2()

    @pl.loop(0, slots // rows)
    def _(i):
        at = pl.ds(pl.multiple_of(i * rows, rows), rows)
        g, b = gp[at, :], bh[at, :]
        s = jax.nn.sigmoid(g)
        pre[at, pl.ds(0, ff)] = (b * up[at, :] * s * (1.0 + g * (1.0 - s))).astype(jnp.bfloat16)
        upv[at, pl.ds(0, ff)] = (b * g * s).astype(jnp.bfloat16)

    f[2].hop2()
    f[3].hop2()
    ext.hop2()

    def back_cols(job):
        cols = job.cols
        value = dot_f32(pre[:, :ff], wg[:, cols]) + dot_f32(upv[:, :ff], wu[:, cols])
        back_part[:, :, :, :, cols] = value.astype(jnp.bfloat16).reshape(lead + (chunk,))
        job.exchange()

    b = back
    back_cols(b[0])
    f[0].hop3()
    back_cols(b[1])
    b[0].hop1()
    f[1].hop3()
    b[0].keep()
    back_cols(b[2])
    b[1].hop1()
    f[2].hop3()
    b[1].keep()
    back_cols(b[3])
    b[2].hop1()
    f[3].hop3()
    ext.hop3()
    b[2].keep()
    for job in [ext] + f:
        job.along(0)
    b[3].hop1()
    b[3].keep()
    b[0].hop2()
    b[1].hop2()
    for stage in range(1, depth - 1):
        for job in [ext] + f:
            job.along(stage)
    b[2].hop2()
    b[3].hop2()
    for job in b:
        job.hop3()
        job.along(0)
    for stage in range(1, depth - 1):
        for job in b:
            job.along(stage)
    for src, dst in ((hid, hid_t), (pre, pre_t), (upv, upv_t)):
        dst[...] = src[...].T[:ff]
    for job in [ext] + forward:
        job.home()
    lane = lax.broadcasted_iota(jnp.int32, (count, LANES), 1)
    cols = gate_cols[...] + pltpu.roll(gate_cols[...], LANES // 2, 1)
    routing = rt[...].astype(jnp.float32)
    grads = jnp.zeros((count, LANES), jnp.float32)
    for k in range(top):
        hit = (routing[:, k : k + 1] == lane.astype(jnp.float32)) & (lane < LANES // 2)
        grads = jnp.where(lane == k, jnp.sum(jnp.where(hit, cols, 0.0), axis=1, keepdims=True), grads)
    square[:count, :] = grads
    gate_grad[...] = square[...].T[: gate_grad.shape[0]]
    for job in back:
        job.home()
    net.finish()


def layer(experts, group, top, capacity, routes, route_gates, tokens, cotangent, w_gate, w_up, w_down):
    depth = experts // 4
    count, width = tokens.shape
    ff = w_gate.shape[1]
    span = depth * capacity
    slots = group * 4 * span
    wide = -(-ff // LANES) * LANES
    bf16, f32 = jnp.bfloat16, jnp.float32
    blocks = (group, 2, 2, span)
    scratch = [
        pltpu.VMEM((ff, width), bf16), pltpu.VMEM((ff, width), bf16), pltpu.VMEM((ff, width), bf16),
        pltpu.VMEM(blocks + (LANES,), bf16), pltpu.VMEM(blocks + (width,), bf16),
        pltpu.VMEM((4, 2, depth * count, LANES), bf16), pltpu.VMEM((slots, LANES), f32),
        pltpu.VMEM((slots, ff), f32), pltpu.VMEM((slots, ff), f32), pltpu.VMEM((slots, ff), f32),
        pltpu.VMEM((slots, wide), bf16), pltpu.VMEM((slots, wide), bf16), pltpu.VMEM((slots, wide), bf16),
        pltpu.VMEM(blocks + (LANES,), bf16), pltpu.VMEM(blocks + (width,), bf16), pltpu.VMEM(blocks + (width,), bf16),
        pltpu.VMEM((slots, LANES), f32), pltpu.VMEM((count, LANES), f32),
    ]
    copies = dispatch_copies(depth, group) + jobs_copies(depth, group)
    return pl.pallas_call(
        functools.partial(layer_kernel, depth, group, top),
        out_shape=[
            jax.ShapeDtypeStruct((count, width), bf16),
            jax.ShapeDtypeStruct((count, width), bf16),
            jax.ShapeDtypeStruct((8, LANES), f32),
            jax.ShapeDtypeStruct(blocks + (width,), bf16),
            jax.ShapeDtypeStruct(blocks + (width,), bf16),
        ] + [jax.ShapeDtypeStruct((ff, slots), bf16)] * 3,
        in_specs=[VMEM_SPEC] * 2 + [ANY_SPEC] * 5,
        out_specs=[VMEM_SPEC] * 8,
        scratch_shapes=scratch
        + dispatch_scratch(depth, count, span, width)
        + jobs_scratch(depth, group, count, span, width)
        + [pltpu.VMEM((count, LANES), bf16), pltpu.VMEM((LANES, LANES), f32)]
        + [pltpu.SemaphoreType.DMA((3,)), pltpu.SemaphoreType.DMA((3,))]
        + semaphores(copies),
        compiler_params=pltpu.CompilerParams(
            collective_id=2, has_side_effects=True, vmem_limit_bytes=VMEM_LIMIT
        ),
    )(routes.T, route_gates.T, tokens, cotangent, w_gate, w_up, w_down)


def weight_kernel(hid_t, pre_t, upv_t, rows_in, rows_back, mixed_in, token_in, route_in, down, gate, up, mixed, token_grad, route_grad):
    down[0] = dot_f32(hid_t[...], rows_back[...])
    gate[0] = dot_f32(pre_t[...], rows_in[...])
    up[0] = dot_f32(upv_t[...], rows_in[...])
    mixed[...] = mixed_in[...]
    token_grad[...] = token_in[...]
    route_grad[...] = route_in[: route_grad.shape[0], : route_grad.shape[1]]


def weight_grads(top, hid_t, pre_t, upv_t, rows_in, rows_back, mixed, token_grad, route_grad):
    ff, slots = hid_t.shape
    count, width = mixed.shape
    chunk = 256
    whole = lambda array: pl.BlockSpec(array.shape, lambda i: (0, 0))
    columns = lambda array: pl.BlockSpec((array.shape[0], chunk), lambda i: (0, i))
    wide = pl.BlockSpec((1, ff, chunk), lambda i: (0, 0, i))
    grads = jax.ShapeDtypeStruct((1, ff, width), jnp.float32)
    route = jax.ShapeDtypeStruct((top, count), jnp.float32)
    return pl.pallas_call(
        weight_kernel,
        grid=(width // chunk,),
        out_shape=[grads, grads, grads, mixed, token_grad, route],
        in_specs=[whole(hid_t)] * 3 + [columns(rows_in)] * 2 + [columns(mixed)] * 2 + [whole(route_grad)],
        out_specs=[wide] * 3 + [columns(mixed)] * 2 + [whole(route)],
        cost_estimate=pl.CostEstimate(
            flops=6 * slots * ff * width, bytes_accessed=12 * ff * width, transcendentals=0
        ),
        compiler_params=pltpu.CompilerParams(vmem_limit_bytes=VMEM_LIMIT),
    )(hid_t, pre_t, upv_t, rows_in, rows_back, mixed, token_grad, route_grad)


def per_device(tokens, cotangent, route_gates, routes, w_gate, w_up, w_down):
    experts, group = lax.axis_size("expert"), lax.axis_size("dp")
    token_count, top_count = routes.shape
    width = tokens.shape[1]
    capacity = max(2, token_count * top_count * 4 // (3 * experts))
    slots = experts * group * capacity
    gate_shard, up_shard, down_shard = (w_gate[0], w_up[0], w_down[0])
    me = lax.axis_index("expert")

    if 2 * slots * width * tokens.dtype.itemsize <= FUSED_LIMIT:
        mixed, token_grad, gate_grad, rows_in, rows_back, hid_t, pre_t, upv_t = layer(
            experts, group, top_count, capacity, routes, route_gates, tokens, cotangent, w_gate, w_up, w_down
        )
        rows_in, rows_back = rows_in.reshape(slots, width), rows_back.reshape(slots, width)
        grad_down, grad_gate, grad_up, mixed, token_grad, gate_grad = weight_grads(
            top_count, hid_t, pre_t, upv_t, rows_in, rows_back, mixed, token_grad, gate_grad
        )
        return (mixed, token_grad, gate_grad.T, grad_gate, grad_up, grad_down)
    routing = jnp.concatenate([routes.astype(jnp.bfloat16), route_gates], axis=1)
    routing = jnp.pad(routing, ((0, 0), (0, LANES - 2 * top_count)))
    row_rt, row_tok, row_cot, tabs = dispatch(experts, group, top_count, capacity, routing, tokens, cotangent)
    shape = row_tok.shape
    row_rt = row_rt.reshape(slots, LANES).astype(jnp.float32)
    rows_in, rows_cot = row_tok.reshape(slots, width), row_cot.reshape(slots, width)
    named = row_rt[:, :top_count] == me.astype(jnp.float32)
    row_gate = jnp.sum(jnp.where(named, row_rt[:, top_count : 2 * top_count], 0.0), axis=1)[:, None]

    gate_pre = dot_f32(rows_in, gate_shard, INNER)
    up_pre = dot_f32(rows_in, up_shard, INNER)
    sig = jax.nn.sigmoid(gate_pre)
    hidden = (gate_pre * sig * up_pre).astype(jnp.bfloat16)
    out_rows = dot_f32(hidden, down_shard)
    row_grad = jnp.sum(out_rows * rows_cot.astype(jnp.float32), axis=1)[:, None]
    out_part = (out_rows * row_gate).astype(jnp.bfloat16)
    lane = jnp.arange(LANES, dtype=jnp.int32)[None, :]
    row_high = row_grad.astype(jnp.bfloat16)
    row_low = (row_grad - row_high.astype(jnp.float32)).astype(jnp.bfloat16)
    zero = jnp.zeros((), jnp.bfloat16)
    grad_cols = jnp.where(lane == me, row_high, jnp.where(lane == LANES // 2 + me, row_low, zero))
    rows_back = (rows_cot.astype(jnp.float32) * row_gate).astype(jnp.bfloat16)
    back_hidden = dot_f32(rows_back, down_shard, INNER)
    grad_pre = (back_hidden * up_pre * sig * (1.0 + gate_pre * (1.0 - sig))).astype(jnp.bfloat16)
    grad_upv = (back_hidden * gate_pre * sig).astype(jnp.bfloat16)
    back_part = (dot_f32(grad_pre, gate_shard) + dot_f32(grad_upv, up_shard)).astype(jnp.bfloat16)
    gate_cols, mixed, token_grad = combine(
        experts, group, capacity, token_count, tabs,
        [grad_cols.reshape(shape[:4] + (LANES,)), out_part.reshape(shape), back_part.reshape(shape)],
    )
    grad_down = dot_f32(hidden, rows_back, OUTER)
    grad_gate = dot_f32(grad_pre, rows_in, OUTER)
    grad_up = dot_f32(grad_upv, rows_in, OUTER)
    column = lane[:, None, :] % (LANES // 2)
    gate_grad = jnp.sum(jnp.where(routes[:, :, None] == column, gate_cols[:, None, :], 0.0), axis=2)
    return (mixed, token_grad, gate_grad, grad_gate[None], grad_up[None], grad_down[None])


def solution(mesh):
    row = P(("expert", "dp"), None)
    wide = P("expert", "dp", None)
    return jax.shard_map(
        per_device,
        mesh=mesh,
        in_specs=(row, row, row, row, wide, wide, wide),
        out_specs=(row, row, row, wide, wide, wide),
        check_vma=False,
    )
```
